32 devices in a mesh: group: 4 (over x, core), seq: 8 (over z, y).
Axes of the slice: x: 2, y: 2, z: 4, core: 2. Of those that a mesh axis runs over, the one named last changes fastest.
Arguments:
- tokens: bfloat16 [4, 1024, 2048], P('group', 'seq'), may hold values from -6 to 6
- norm_gain: bfloat16 [2048], replicated, may hold values from 0.25 to 1.75
- w_qkv: bfloat16 [2048, 1920], P(('group', 'seq')), may hold values from -1.767767 to 1.767767
- prefix_kv: bfloat16 [4, 512, 640], P('group', 'seq'), may hold values from -12 to 12
- segments: int32 [4, 1024], P('group', 'seq'), may hold values from 0 to 3, never falling along the last dimension, each value on 1 to 512 neighbouring positions
Outputs:
- context: bfloat16 [4, 1024, 1280], P('group', 'seq')
The draws below stay inside these ranges and needn't reach their ends.
Inputs may be any that keep to these rules, and one draw needn't show every extreme that they name: `segments`: within each group's 1024 suffix tokens the request numbers never fall; every request holds 1 to 512 tokens and one holds exactly 512.
All inputs are finite; a program needn't handle non-finite values.
Results may differ from the reference program's by a relative error of at most 0.0096.
Values may be sent and summed in bfloat16 or wider, within the bound.
No kernel may reach another device: no remote copies, remote signals or barrier semaphores. Data moves between devices by JAX's collectives and lax.ppermute only.
A program may use at most 64 MiB of HBM per device.

```python
import math
import jax
import jax.numpy as jnp
import numpy as np
from jax import lax

D = 2048
HD = 64
QW = 1280
KVW = 320
SUF = 1024
PREFIX = 512
REQS = 4
MOST = 512
GROUPS = 4


def draw_w_qkv(key, part):
    first_key, second_key = jax.random.split(key, 2)
    column_total = QW + 2 * KVW
    spread = (D // 4) ** (-0.5)
    base = jnp.clip(jax.random.normal(first_key, (D, column_total), jnp.float32), -4.0, 4.0)
    base = base * spread
    query_heads = QW // HD
    key_heads = KVW // HD
    repeats = QW // KVW
    ranks = jax.random.permutation(second_key, query_heads).astype(jnp.float32)
    strength = 9.0 * jnp.maximum(ranks - (query_heads - 6.0), 0.0) / 5.0
    key_columns = base[:, QW:QW + KVW].reshape(D, key_heads, 1, HD)
    aligned = jnp.broadcast_to(key_columns, (D, key_heads, repeats, HD)).reshape(D, QW)
    head_scale = jnp.repeat(strength, HD)
    query_columns = base[:, :QW] + aligned * head_scale[None, :]
    return jnp.concatenate([query_columns, base[:, QW:]], axis=1).astype(jnp.bfloat16)


def block_scale(own_key, shape, cuts, low, top_value):
    def one(dim, parts):
        steps = jax.random.uniform(jax.random.fold_in(jax.random.fold_in(own_key, 6), dim), (parts,), jnp.float32, low / len(cuts), top_value / len(cuts))
        return jnp.repeat(jnp.exp(steps), shape[dim] // parts).reshape((-1,) + (1,) * (len(shape) - dim - 1))

    factor_of = one(*cuts[0])
    for cut in cuts[1:]:
        factor_of = factor_of * one(*cut)
    return factor_of


def split_up(amount, total, bound, lean):
    loads = [(1 << 20) // math.isqrt(rank ** lean) + 1 for rank in range(2, amount + 1)]
    surplus, holding = total - bound - (amount - 1), [1] * (amount - 1)
    while surplus > 0:
        movable = [i for i in range(amount - 1) if holding[i] < bound]
        whole, left = sum([loads[i] for i in movable]), surplus
        for i in movable:
            more = min(bound - holding[i], max(1, left * loads[i] // whole), surplus)
            holding[i] = holding[i] + more
            surplus = surplus - more
    return np.array([bound] + holding)


def uneven_parts(own_key, amount, total, limit, skew):
    if amount == 2:
        one = jax.random.randint(own_key, (), max(1, total - limit), min(limit, total - 1) + 1)
        return jnp.stack([one, total - one])
    lengths = jnp.asarray(split_up(amount, total, limit, skew), jnp.int32)
    twos = (amount - 1) // 2
    donor, sink = lengths[1:1 + 2 * twos:2], lengths[2:2 + 2 * twos:2]
    slack = jnp.minimum(donor - 1, limit - sink)
    moved = jax.random.randint(jax.random.fold_in(own_key, 1), (twos,), 0, 1 << 20) % (slack + 1)
    lengths = lengths.at[1:1 + 2 * twos:2].set(donor - moved).at[2:2 + 2 * twos:2].set(sink + moved)
    return lengths[jax.random.permutation(jax.random.fold_in(own_key, 2), amount)]


def noise(key, dims, scale, limit, pieces=(), kind=jnp.bfloat16):
    level = block_scale(key, dims, pieces, -0.22, 0.18) if pieces else 1.0
    values = jax.random.normal(key, dims, jnp.float32) * scale * level
    return jnp.minimum(jnp.maximum(values, -limit), limit).astype(kind)


def setup_inputs(seed: int = 0) -> dict:
    key_of = jax.random.split(jax.random.key(seed), 6)
    return {
        "tokens": noise(key_of[0], (GROUPS, SUF, D), 1.0, 6.0, ((0, 4), (1, 8))),
        "norm_gain": jnp.clip(1.0 + 0.15 * jax.random.normal(key_of[1], (D,), jnp.float32), 0.25, 1.75).astype(jnp.bfloat16),
        "w_qkv": draw_w_qkv(jax.random.fold_in(key_of[5], 71), 0),
        "prefix_kv": noise(key_of[3], (GROUPS, PREFIX, 2 * KVW), 2.0, 12.0, ((0, 4), (1, 8))),
        "segments": jax.vmap(lambda own: jnp.searchsorted(jnp.cumsum(uneven_parts(own, REQS, SUF, MOST, 2)), jnp.arange(SUF), side="right"))(jax.random.split(key_of[4], GROUPS)).reshape((GROUPS, SUF)).astype(jnp.int32),
    }


def attend(queries, keyvals, visible):
    count = queries.shape[0]
    width = keyvals.shape[0]
    heads = KVW // HD
    query_heads = queries.astype(jnp.float32).reshape(count, heads, QW // KVW, HD)
    key_part = keyvals[:, :KVW].astype(jnp.float32).reshape(width, heads, HD)
    value_part = keyvals[:, KVW:].astype(jnp.float32).reshape(width, heads, HD)
    scores = jnp.einsum('tgrd,ngd->tgrn', query_heads, key_part) * 0.125
    wide_mask = visible[:, None, None, :]
    scores = jnp.where(wide_mask, scores, jnp.float32(-1e+30))
    row_max = lax.optimization_barrier(jnp.max(scores, axis=-1, keepdims=True))
    probability = jnp.where(wide_mask, jnp.exp(scores - row_max), jnp.float32(0.0))
    denominator = lax.optimization_barrier(jnp.sum(probability, axis=-1))
    rounded = lax.optimization_barrier(probability.astype(jnp.bfloat16))
    numerator = jnp.einsum('tgrn,ngd->tgrd', rounded.astype(jnp.float32), value_part)
    return (numerator / denominator[..., None]).reshape(count, QW).astype(jnp.bfloat16)

def reference(tokens, norm_gain, w_qkv, prefix_kv, segments):
    block_rows = math.gcd(SUF, 512)
    block_count = SUF // block_rows

    def one_group(items):
        inputs, cache, seg_ids = items
        values_f = inputs.astype(jnp.float32)
        mean_square = lax.optimization_barrier(jnp.mean(values_f * values_f, axis=-1, keepdims=True))
        normed = (values_f * lax.rsqrt(mean_square + 1e-05) * norm_gain.astype(jnp.float32)).astype(jnp.bfloat16)
        projected = jnp.dot(normed, w_qkv, preferred_element_type=jnp.float32).astype(jnp.bfloat16)
        queries = projected[:, :QW]
        all_keys = jnp.concatenate([cache, projected[:, QW:]], axis=0)
        key_pos = jnp.arange(SUF, dtype=jnp.int32)

        def one_block(block_index):
            first_row = (block_index * block_rows).astype(jnp.int32)
            block_q = lax.dynamic_slice_in_dim(queries, first_row, block_rows, 0)
            query_seg = lax.dynamic_slice_in_dim(seg_ids, first_row, block_rows, 0)
            query_pos = first_row + jnp.arange(block_rows, dtype=jnp.int32)
            suffix_mask = (seg_ids[None, :] == query_seg[:, None]) & (key_pos[None, :] <= query_pos[:, None])
            visible = jnp.concatenate([jnp.ones((block_rows, PREFIX), dtype=bool), suffix_mask], axis=1)
            return attend(block_q, all_keys, visible)
        blocks = lax.map(one_block, jnp.arange(block_count, dtype=jnp.int32))
        return blocks.reshape(SUF, QW)
    return lax.map(one_group, (tokens, prefix_kv, segments))
```

```python
import functools

import jax
import jax.numpy as jnp
from jax import lax
from jax.experimental import pallas as pl
from jax.experimental.pallas import tpu as pltpu
from jax.sharding import Mesh, PartitionSpec as P

HD = 64
QW = 1280
KVW = 320
KEY_HEADS = KVW // HD
REPEATS = QW // KVW
QH = QW // 2
NEG = -1e30
SMALL = 4
F32 = jnp.float32
BF16 = jnp.bfloat16


def rms_norm(inputs, norm_gain):
    values = inputs.astype(F32)
    mean_square = jnp.mean(values * values, axis=-1, keepdims=True)
    return (values * lax.rsqrt(mean_square + 1e-05) * norm_gain.astype(F32)).astype(BF16)


def swap(x, axis):
    return lax.ppermute(x, axis, [(0, 1), (1, 0)])


def z_swap(x, distance):
    return lax.ppermute(x, "z", [(i, i ^ distance) for i in range(4)])


def plane(piece, ident):
    from_x, from_y = swap(piece, "gx"), swap(piece, "y")
    half = piece.shape[0] // 2
    low = swap(from_x[:half], "y")
    high = swap(from_y[half:], "gx")
    return from_x, from_y, low, high


def project_kernel(scale, n_pieces, places, pos, own, other, *refs):
    pieces, (mine, theirs), (weights, sems) = refs[:n_pieces], refs[n_pieces:n_pieces + 2], refs[n_pieces + 2:]
    copies = []
    for i, (piece, row, spot) in enumerate(places):
        start = pl.multiple_of(pos[spot], 64)
        copies.append(
            pltpu.make_async_copy(pieces[piece].at[pl.ds(row, 64), :], weights.at[pl.ds(start, 64), :], sems.at[i])
        )
    for copy in copies:
        copy.start()
    for copy in copies:
        copy.wait()
    for source, target in ((own, mine), (other, theirs)):
        result = jnp.dot(source[...], weights[...], preferred_element_type=F32).astype(BF16)
        target[...] = result if scale is None else result * jnp.asarray(scale, BF16)


def project(own, other, pieces, places, pos, scale):
    rows, depth = own.shape
    width = pieces[0].shape[1]
    vmem = pl.BlockSpec(memory_space=pltpu.VMEM)
    return pl.pallas_call(
        functools.partial(project_kernel, scale, len(pieces), places),
        out_shape=[jax.ShapeDtypeStruct((rows, width), BF16)] * 2,
        in_specs=[pl.BlockSpec(memory_space=pltpu.SMEM), vmem, vmem]
        + [pl.BlockSpec(memory_space=pl.ANY)] * len(pieces),
        out_specs=[vmem, vmem],
        scratch_shapes=[pltpu.VMEM((depth, width), BF16), pltpu.SemaphoreType.DMA((len(places),))],
        compiler_params=pltpu.CompilerParams(vmem_limit_bytes=24 << 20),
        cost_estimate=pl.CostEstimate(
            flops=4 * rows * depth * width, bytes_accessed=2 * depth * width + 8 * rows * depth, transcendentals=0
        ),
    )(pos, own, other, *pieces)


def gather_columns(first, second):
    n = first.shape[0]
    own = jnp.concatenate([first, second])
    far = jnp.concatenate([z_swap(own, d) for d in (1, 2, 3)])
    arrays, places = [], []

    def add(array, blocks):
        for i, (dz, half, dx, dy) in enumerate(blocks):
            places.append((len(arrays), n * i, ((dz * 2 + dx) * 2 + dy) * 2 + half))
        arrays.append(array)

    for piece, zs in ((own, (0,)), (far, (1, 2, 3))):
        blocks = [(dz, half) for dz in zs for half in (0, 1)]
        mid = len(blocks) // 2
        from_x, from_y, low, high = plane(piece, None)
        add(piece, [b + (0, 0) for b in blocks])
        add(from_x, [b + (1, 0) for b in blocks])
        add(from_y, [b + (0, 1) for b in blocks])
        add(low, [b + (1, 1) for b in blocks[:mid]])
        add(high, [b + (1, 1) for b in blocks[mid:]])
    return arrays, places


def attend_kernel(earlier, scalars, q_mine, q_theirs, prefix, seg_col, *refs):
    blocks, out, q_all = refs[:earlier + 1], refs[earlier + 1], refs[earlier + 2]
    core, index = scalars[0], scalars[1]
    rows = q_mine.shape[0]
    low = core == 0
    q_all[:, :QH] = jnp.where(low, q_mine[...], q_theirs[...])
    q_all[:, QH:] = jnp.where(low, q_theirs[...], q_mine[...])
    biases = []
    q_seg = seg_col[...]
    for distance in range(earlier, -1, -1):
        k_seg = blocks[distance][rows:rows + 1, :rows].astype(F32)
        seen = q_seg == k_seg
        if distance == 0:
            q_at = lax.broadcasted_iota(jnp.int32, (rows, rows), 0)
            k_at = lax.broadcasted_iota(jnp.int32, (rows, rows), 1)
            seen = seen & (k_at <= q_at)
            biases.append(jnp.where(seen, 0.0, NEG))
        else:
            biases.append(jnp.where(seen, jnp.where(index >= distance, 0.0, NEG), NEG))
    bias = jnp.concatenate(biases, axis=1)
    bias = jnp.concatenate([bias] * REPEATS, axis=0)
    for head in range(KEY_HEADS):
        cols, vcols = slice(head * HD, (head + 1) * HD), slice(KVW + head * HD, KVW + (head + 1) * HD)
        base = head * REPEATS * HD
        queries = jnp.concatenate([q_all[:, base + r * HD:base + (r + 1) * HD] for r in range(REPEATS)], axis=0)
        keys = jnp.concatenate([blocks[d][:rows, cols] for d in range(earlier, -1, -1)], axis=0)
        values = jnp.concatenate([blocks[d][:rows, vcols] for d in range(earlier, -1, -1)], axis=0)
        contract = (((1,), (1,)), ((), ()))
        s_pre = lax.dot_general(queries, prefix[:, cols], contract, preferred_element_type=F32)
        s_suf = lax.dot_general(queries, keys, contract, preferred_element_type=F32) + bias
        top = jnp.maximum(jnp.max(s_pre, axis=-1, keepdims=True), jnp.max(s_suf, axis=-1, keepdims=True))
        p_pre, p_suf = jnp.exp(s_pre - top), jnp.exp(s_suf - top)
        total = jnp.sum(p_pre, axis=-1, keepdims=True) + jnp.sum(p_suf, axis=-1, keepdims=True)
        numerator = jnp.dot(p_pre.astype(BF16), prefix[:, vcols], preferred_element_type=F32)
        numerator += jnp.dot(p_suf.astype(BF16), values, preferred_element_type=F32)
        context = (numerator / total).astype(BF16)
        for r in range(REPEATS):
            out[:, base + r * HD:base + (r + 1) * HD] = context[r * rows:(r + 1) * rows]


def attend(q_mine, q_theirs, prefix, seg_col, blocks, scalars):
    rows = q_mine.shape[0]
    earlier = len(blocks) - 1
    vmem = pl.BlockSpec(memory_space=pltpu.VMEM)
    keys = prefix.shape[0] + rows * (earlier + 1)
    return pl.pallas_call(
        functools.partial(attend_kernel, earlier),
        out_shape=jax.ShapeDtypeStruct((rows, QW), BF16),
        in_specs=[pl.BlockSpec(memory_space=pltpu.SMEM)] + [vmem] * (4 + len(blocks)),
        out_specs=vmem,
        scratch_shapes=[pltpu.VMEM((rows, QW), BF16)],
        compiler_params=pltpu.CompilerParams(vmem_limit_bytes=40 << 20),
        cost_estimate=pl.CostEstimate(
            flops=4 * rows * keys * QW, bytes_accessed=4 * keys * KVW, transcendentals=rows * keys * QW // HD
        ),
    )(scalars, q_mine, q_theirs, prefix, seg_col, *blocks)


def swap_body(tokens, norm_gain, w_qkv, prefix_kv, segments):
    inputs, seg_ids, own_prefix = tokens[0], segments[0], prefix_kv[0]
    rows = inputs.shape[0]
    gx, core, z, y = (lax.axis_index(a) for a in ("gx", "core", "z", "y"))
    z_count, y_count = lax.axis_size("z"), lax.axis_size("y")
    index = z * y_count + y
    depth = w_qkv.shape[0]

    kv_own = lax.dynamic_slice_in_dim(w_qkv, QW + core * KVW, KVW, 1)
    kv_send = lax.dynamic_slice_in_dim(w_qkv, QW + (1 - core) * KVW, KVW, 1)
    q_own = lax.dynamic_slice_in_dim(w_qkv, core * QH, QH, 1)
    q_send = lax.dynamic_slice_in_dim(w_qkv, (1 - core) * QH, QH, 1)
    kv_got, q_got = swap(kv_send, "core"), swap(q_send, "core")

    spots = []
    for dz in range(4):
        for dx in range(2):
            for dy in range(2):
                for half in range(2):
                    block = (((gx ^ dx) * 2 + (core ^ half)) * z_count + (z ^ dz)) * y_count + (y ^ dy)
                    spots.append(block * depth)
    pos = jnp.stack(spots).astype(jnp.int32)

    kv_pieces, kv_places = gather_columns(kv_own, kv_got)
    q_pieces, q_places = gather_columns(q_own, q_got)

    normed = rms_norm(inputs, norm_gain)
    normed_sibling = swap(normed, "core")

    kv_mine, kv_theirs = project(normed, normed_sibling, kv_pieces, kv_places, pos, None)
    kv_other = swap(kv_theirs, "core")
    low = core == 0
    seg_row = jnp.pad(seg_ids.astype(BF16)[None, :], ((0, 7), (0, 2 * KVW - rows)))
    block = jnp.concatenate(
        [
            jnp.concatenate([jnp.where(low, kv_mine, kv_other), jnp.where(low, kv_other, kv_mine)], axis=1),
            seg_row,
        ],
        axis=0,
    )
    seq_count = z_count * y_count
    earlier = -(-(seq_count // 2 * rows - 1) // rows)
    blocks = [block] + [
        lax.ppermute(block, ("z", "y"), [(s, s + d) for s in range(seq_count - d)]) for d in range(1, earlier + 1)
    ]

    q_mine, q_theirs = project(normed, normed_sibling, q_pieces, q_places, pos, 0.125)
    q_other = swap(q_theirs, "core")

    line = jnp.concatenate([own_prefix] + [z_swap(own_prefix, d) for d in (1, 2, 3)])
    prefix = jnp.concatenate([line, swap(line, "y")])

    scalars = jnp.stack([core, index]).astype(jnp.int32)
    context = attend(q_mine, q_other, prefix, seg_ids.astype(F32)[:, None], blocks, scalars)
    return context[None]


def gather_body(tokens, norm_gain, w_qkv, prefix_kv, segments):
    inputs, seg_ids = tokens[0], segments[0]
    rows = inputs.shape[0]
    normed = rms_norm(inputs, norm_gain)
    weights = lax.all_gather(w_qkv, ("gx", "core", "z", "y"), axis=0, tiled=True)
    projected = jnp.dot(normed, weights, preferred_element_type=F32).astype(BF16)
    queries = projected[:, :QW].reshape(rows, KEY_HEADS, REPEATS, HD)

    def absorb(state, keyvals, visible):
        running_max, denominator, numerator = state
        count = keyvals.shape[0]
        key_part = keyvals[:, :KVW].reshape(count, KEY_HEADS, HD)
        value_part = keyvals[:, KVW:].reshape(count, KEY_HEADS, HD)
        scores = jnp.einsum("tgrd,ngd->tgrn", queries, key_part, preferred_element_type=F32) * 0.125
        if visible is not None:
            scores = jnp.where(visible[:, None, None, :], scores, F32(NEG))
        new_max = jnp.maximum(running_max, jnp.max(scores, axis=-1))
        probability = jnp.exp(scores - new_max[..., None])
        if visible is not None:
            probability = jnp.where(visible[:, None, None, :], probability, F32(0.0))
        factor = jnp.exp(running_max - new_max)
        denominator = denominator * factor + jnp.sum(probability, axis=-1)
        numerator = numerator * factor[..., None] + jnp.einsum(
            "tgrn,ngd->tgrd", probability.astype(BF16), value_part, preferred_element_type=F32
        )
        return new_max, denominator, numerator

    def sweep(state, keyvals, key_seg):
        length = min(keyvals.shape[0], 512)

        def step(i, running):
            start = i * length
            part = lax.dynamic_slice_in_dim(keyvals, start, length, 0)
            if key_seg is None:
                return absorb(running, part, None)
            seg_part = lax.dynamic_slice_in_dim(key_seg, start, length, 0)
            key_pos = start + jnp.arange(length, dtype=jnp.int32)
            visible = (seg_part[None, :] == seg_ids[:, None]) & (key_pos[None, :] <= query_pos[:, None])
            return absorb(running, part, visible)

        return lax.fori_loop(0, keyvals.shape[0] // length, step, state)

    query_pos = lax.axis_index(("z", "y")) * rows + jnp.arange(rows, dtype=jnp.int32)
    state = (
        jnp.full((rows, KEY_HEADS, REPEATS), NEG, F32),
        jnp.zeros((rows, KEY_HEADS, REPEATS), F32),
        jnp.zeros((rows, KEY_HEADS, REPEATS, HD), F32),
    )
    along = functools.partial(lax.all_gather, axis_name=("z", "y"), axis=0, tiled=True)
    state = sweep(state, along(prefix_kv[0]), None)
    _, denominator, numerator = sweep(state, along(projected[:, QW:]), along(seg_ids))
    return (numerator / denominator[..., None]).reshape(rows, QW).astype(BF16)[None]


def solution(mesh):
    groups, seqs = mesh.shape["group"], mesh.shape["seq"]
    chips, z_count = groups // 2, seqs // 2
    fine = Mesh(mesh.devices.reshape(chips, 2, z_count, 2), ("gx", "core", "z", "y"))
    group, seq = ("gx", "core"), ("z", "y")
    short = chips == 2 and z_count == SMALL
    return jax.shard_map(
        swap_body if short else gather_body,
        mesh=fine,
        in_specs=(P(group, seq, None), P(), P(group + seq, None), P(group, seq, None), P(group, seq)),
        out_specs=P(group, seq, None),
        check_vma=False,
    )
```

```python
import functools

import jax
import jax.numpy as jnp
from jax import lax
from jax.experimental import pallas as pl
from jax.experimental.pallas import tpu as pltpu
from jax.sharding import Mesh, PartitionSpec as P

HD = 64
QW = 1280
KVW = 320
KEY_HEADS = KVW // HD
REPEATS = QW // KVW
QH, QQ = QW // 2, QW // 4
NEG = -1e30
SMALL = 4
F32 = jnp.float32
BF16 = jnp.bfloat16


def rms_norm(inputs, norm_gain):
    values = inputs.astype(F32)
    mean_square = jnp.mean(values * values, axis=-1, keepdims=True)
    return (values * lax.rsqrt(mean_square + 1e-05) * norm_gain.astype(F32)).astype(BF16)


def swap(x, axis):
    return lax.ppermute(x, axis, [(0, 1), (1, 0)])


def z_swap(x, distance):
    return lax.ppermute(x, "z", [(i, i ^ distance) for i in range(4)])


def sides(piece):
    return swap(piece, "gx"), swap(piece, "y")


def corner(near_sides, far_sides):
    (near_x, near_y), (far_x, far_y) = near_sides, far_sides
    near, far = near_x.shape[0] // 2, far_x.shape[0] // 2
    low = swap(jnp.concatenate([near_x[:near], far_x[:far]]), "y")
    high = swap(jnp.concatenate([near_y[near:], far_y[far:]]), "gx")
    return low, high


def order_kernel(order, bits, *refs):
    sources, out = refs[:-1], refs[-1]
    at = 0
    for source in sources:
        rows, depth = source.shape
        x = source[...]
        for bit in range((depth // 64).bit_length() - 1):
            span = 64 << bit
            parts = [x[:, (i ^ 1) * span:((i ^ 1) + 1) * span] for i in range(depth // span)]
            x = jnp.where(bits[bit] == 1, jnp.concatenate(parts, axis=1), x)
        out[at:at + rows, :] = jnp.concatenate([x[:, b * 64:(b + 1) * 64] for b in order], axis=1)
        at += rows


def order_features(sources, order, bits):
    depth = sources[0].shape[1]
    rows = sum(x.shape[0] for x in sources)
    vmem = pl.BlockSpec(memory_space=pltpu.VMEM)
    return pl.pallas_call(
        functools.partial(order_kernel, order),
        out_shape=jax.ShapeDtypeStruct((rows, depth), BF16),
        in_specs=[pl.BlockSpec(memory_space=pltpu.SMEM)] + [vmem] * len(sources),
        out_specs=vmem,
        compiler_params=pltpu.CompilerParams(vmem_limit_bytes=24 << 20),
        cost_estimate=pl.CostEstimate(flops=0, bytes_accessed=4 * rows * depth, transcendentals=0),
    )(bits, *sources)


def add_products(total, features, at, pieces, side):
    for piece in pieces:
        rows, width = piece.shape[0], piece.shape[1] // side
        for i in range(side):
            term = jnp.dot(
                features[:, at:at + rows], piece[:, i * width:(i + 1) * width], preferred_element_type=F32
            )
            total = term if total is None else total + term
            at += rows
    return total


def first_kernel(side, features, *refs):
    pieces, out = refs[:-1], refs[-1]
    out[...] = add_products(None, features, 0, pieces, side)


def last_kernel(side, at, n_late, scale, features, so_far, *refs):
    late, outs = refs[:n_late], refs[n_late:]
    result = add_products(so_far[...], features, at, late, side).astype(BF16)
    if scale is not None:
        result = result * jnp.asarray(scale, BF16)
    rows = outs[0].shape[0]
    for i, out in enumerate(outs):
        out[...] = result[i * rows:(i + 1) * rows]


def project(features, pieces, side, parts, scale, late):
    rows, depth = features.shape
    width = pieces[0].shape[1] // side
    vmem = pl.BlockSpec(memory_space=pltpu.VMEM)
    early = len(pieces) - late
    params = pltpu.CompilerParams(vmem_limit_bytes=24 << 20)
    done = side * sum(p.shape[0] for p in pieces[:early])

    def cost(deep):
        return pl.CostEstimate(flops=2 * rows * deep * width, bytes_accessed=2 * deep * (width + rows), transcendentals=0)

    so_far = pl.pallas_call(
        functools.partial(first_kernel, side),
        out_shape=jax.ShapeDtypeStruct((rows, width), F32),
        in_specs=[vmem] * (1 + early),
        out_specs=vmem,
        compiler_params=params,
        cost_estimate=cost(done),
    )(features, *pieces[:early])
    return pl.pallas_call(
        functools.partial(last_kernel, side, done, late, scale),
        out_shape=[jax.ShapeDtypeStruct((rows // parts, width), BF16)] * parts,
        in_specs=[vmem] * (2 + late),
        out_specs=[vmem] * parts,
        compiler_params=params,
        cost_estimate=cost(depth - done),
    )(features, so_far, *pieces[early:])


def piece_order(near, far):
    pieces = [(dx, dy, some) for some in (near, far) for dx, dy in ((0, 0), (1, 0), (0, 1))]
    pieces += [(1, 1, near[:len(near) // 2] + far[:len(far) // 2]), (1, 1, near[len(near) // 2:] + far[len(far) // 2:])]
    return [[((dx * 2 + half) * 4 + dz) * 2 + dy for half, dz in some] for dx, dy, some in pieces]


def after(first, *then):
    return lax.optimization_barrier((first,) + then)[1:]


def attend_kernel(earlier, scalars, mine, pair, sibling, diagonal, prefix, seg_col, *refs):
    blocks, out, q_all = refs[:earlier + 1], refs[earlier + 1], refs[earlier + 2]
    quarter = scalars[0]
    rows = mine.shape[0]
    for i, part in enumerate((mine, pair, sibling, diagonal)):
        q_all[quarter ^ i] = part[...]
    biases = []
    q_seg = seg_col[...]
    for i, block in enumerate(blocks):
        k_seg = block[rows:rows + 1, :rows].astype(F32)
        seen = q_seg == k_seg
        if i == 0:
            q_at = lax.broadcasted_iota(jnp.int32, (rows, rows), 0)
            k_at = lax.broadcasted_iota(jnp.int32, (rows, rows), 1)
            seen = seen & (k_at <= q_at)
            biases.append(jnp.where(seen, 0.0, NEG))
        else:
            biases.append(jnp.where(seen, jnp.where(scalars[1 + i] == 0, 0.0, NEG), NEG))
    bias = jnp.concatenate(biases, axis=1)
    bias = jnp.concatenate([bias] * REPEATS, axis=0)
    for head in range(KEY_HEADS):
        cols, vcols = slice(head * HD, (head + 1) * HD), slice(KVW + head * HD, KVW + (head + 1) * HD)
        base = head * REPEATS * HD
        heads = [divmod(head * REPEATS + r, QQ // HD) for r in range(REPEATS)]
        queries = jnp.concatenate([q_all[part, :, h * HD:(h + 1) * HD] for part, h in heads], axis=0)
        keys = jnp.concatenate([block[:rows, cols] for block in blocks], axis=0)
        values = jnp.concatenate([block[:rows, vcols] for block in blocks], axis=0)
        contract = (((1,), (1,)), ((), ()))
        s_pre = lax.dot_general(queries, prefix[:, cols], contract, preferred_element_type=F32)
        s_suf = lax.dot_general(queries, keys, contract, preferred_element_type=F32) + bias
        top = jnp.maximum(jnp.max(s_pre, axis=-1, keepdims=True), jnp.max(s_suf, axis=-1, keepdims=True))
        p_pre, p_suf = jnp.exp(s_pre - top), jnp.exp(s_suf - top)
        total = jnp.sum(p_pre, axis=-1, keepdims=True) + jnp.sum(p_suf, axis=-1, keepdims=True)
        numerator = jnp.dot(p_pre.astype(BF16), prefix[:, vcols], preferred_element_type=F32)
        numerator += jnp.dot(p_suf.astype(BF16), values, preferred_element_type=F32)
        context = (numerator / total).astype(BF16)
        for r in range(REPEATS):
            out[:, base + r * HD:base + (r + 1) * HD] = context[r * rows:(r + 1) * rows]


def attend(quarters, prefix, seg_col, blocks, scalars):
    rows = quarters[0].shape[0]
    earlier = len(blocks) - 1
    vmem = pl.BlockSpec(memory_space=pltpu.VMEM)
    keys = prefix.shape[0] + rows * (earlier + 1)
    return pl.pallas_call(
        functools.partial(attend_kernel, earlier),
        out_shape=jax.ShapeDtypeStruct((rows, QW), BF16),
        in_specs=[pl.BlockSpec(memory_space=pltpu.SMEM)] + [vmem] * (6 + len(blocks)),
        out_specs=vmem,
        scratch_shapes=[pltpu.VMEM((4, rows, QQ), BF16)],
        compiler_params=pltpu.CompilerParams(vmem_limit_bytes=40 << 20),
        cost_estimate=pl.CostEstimate(
            flops=4 * rows * keys * QW, bytes_accessed=4 * keys * KVW, transcendentals=rows * keys * QW // HD
        ),
    )(scalars, *quarters, prefix, seg_col, *blocks)


def swap_body(tokens, norm_gain, w_qkv, prefix_kv, segments):
    inputs, seg_ids, own_prefix = tokens[0], segments[0], prefix_kv[0]
    rows = inputs.shape[0]
    gx, core, z, y = (lax.axis_index(a) for a in ("gx", "core", "z", "y"))
    z_count, y_count = lax.axis_size("z"), lax.axis_size("y")
    index = z * y_count + y
    depth = w_qkv.shape[0]

    def half(of):
        keys = lax.dynamic_slice_in_dim(w_qkv, QW + of * KVW, KVW, 1)
        return jnp.concatenate([lax.dynamic_slice_in_dim(w_qkv, of * QH, QH, 1), keys], axis=1)

    kept, got = half(core), swap(half(1 - core), "core")
    kv_near = jnp.concatenate([kept[:, QH:], got[:, QH:]])
    kv_zs = [z_swap(kv_near, d) for d in (1, 2, 3)]
    kv_near_sides = sides(kv_near)

    pair = z & 1
    kept, got, own_prefix = after(kv_near_sides, kept, got, own_prefix)
    q_rows = jnp.concatenate([kept[:, :QH], got[:, :QH]])
    q_send = lax.dynamic_slice_in_dim(q_rows, (1 - pair) * QQ, QQ, 1)
    q_send = jnp.concatenate([jnp.concatenate([q_send[:depth], q_send[depth:]], axis=1), own_prefix])
    q_got = z_swap(q_send, 1)
    q_keep = lax.dynamic_slice_in_dim(q_rows, pair * QQ, QQ, 1)
    q_got_rows = jnp.concatenate([q_got[:depth, :QQ], q_got[:depth, QQ:]])
    q_near = jnp.concatenate([q_keep, q_got_rows], axis=1)

    kv_far = jnp.concatenate(after(q_got, *kv_zs))
    kv_far_sides = sides(kv_far)

    (normed_in,) = after(kv_near, inputs)
    normed = rms_norm(normed_in, norm_gain)
    normed_sibling = swap(normed, "core")
    number = ((gx * 2 + core) * z_count + z) * y_count + y
    bits = jnp.stack([(number >> i) & 1 for i in range(5)]).astype(jnp.int32)
    kv_order = piece_order([(0, 0), (1, 0)], [(half, dz) for dz in (1, 2, 3) for half in (0, 1)])
    kv_features = order_features([normed, normed_sibling], [b for piece in kv_order for b in piece], bits)

    (q_load,) = after(kv_far, jnp.concatenate([q_near, own_prefix, q_got[depth:]]))
    q_across = z_swap(q_load, 2)
    (normed_out,) = after(kv_far_sides, normed)
    normed_pair = z_swap(normed_out, 1)

    kv_corner = corner(kv_near_sides, after(kv_features, *kv_far_sides))
    kv_pieces = [kv_near, *kv_near_sides, kv_far, *kv_far_sides, *kv_corner]
    kv_mine, kv_theirs = project(kv_features, kv_pieces, 1, 2, None, 2)
    kv_other = swap(kv_theirs, "core")
    q_line = jnp.concatenate([q_near, *after(kv_theirs, q_across[:2 * depth])])
    q_line_x, q_line_y = sides(q_line)
    low = core == 0
    seg_row = jnp.pad(seg_ids.astype(BF16)[None, :], ((0, 7), (0, 2 * KVW - rows)))
    block = jnp.concatenate(
        [
            jnp.concatenate([jnp.where(low, kv_mine, kv_other), jnp.where(low, kv_other, kv_mine)], axis=1),
            seg_row,
        ],
        axis=0,
    )
    upward = [(i, i + 1) for i in range(z_count - 1)]
    two_back = lax.ppermute(block, "z", upward)
    four_back = lax.ppermute(two_back, "z", upward)
    odd_a = swap(two_back, "y")
    odd_b = swap(jnp.where(y == 0, block, four_back), "y")
    blocks = [block, two_back, four_back, odd_a, odd_b]
    distances = [0, 2, 4, 1 + 2 * y, 3 - 2 * y]

    q_late_x, q_late_y = after(two_back, q_line_x[:2 * depth], q_line_y[2 * depth:])
    q_low, q_high = swap(q_late_x, "y"), swap(q_late_y, "gx")
    q_pieces = [q_line, q_line_x, q_line_y, q_low, q_high]
    q_order = []
    for dx, dy, spans in ((0, 0, (0, 2)), (1, 0, (0, 2)), (0, 1, (0, 2)), (1, 1, (0,)), (1, 1, (2,))):
        for pair_bit in (0, 1):
            q_order += [((dx * 2 + half) * 4 + (far ^ pair_bit)) * 2 + dy for far in spans for half in (0, 1)]
    (normed_pair,) = after(block, normed_pair)
    normed_diagonal = swap(normed_pair, "core")
    q_features = order_features([normed, normed_sibling, normed_pair, normed_diagonal], q_order, bits)
    q_mine, q_sibling, q_pair, q_diagonal = project(q_features, q_pieces, 2, 4, 0.125, 2)
    own_got, sibling_got = jnp.split(z_swap(jnp.concatenate([q_pair, q_diagonal]), 1), 2)
    from_sibling = swap(jnp.concatenate([q_sibling, sibling_got]), "core")
    quarters = [q_mine, own_got, *jnp.split(from_sibling, 2)]

    line = jnp.concatenate([own_prefix, q_got[depth:], q_across[2 * depth:]])
    prefix = jnp.concatenate([line, swap(line, "y")])

    scalars = jnp.stack([core * 2 + pair] + [jnp.where(index >= d, 0, 1) for d in distances]).astype(jnp.int32)
    context = attend(quarters, prefix, seg_ids.astype(F32)[:, None], blocks, scalars)
    return context[None]


def gather_body(tokens, norm_gain, w_qkv, prefix_kv, segments):
    inputs, seg_ids = tokens[0], segments[0]
    rows = inputs.shape[0]
    normed = rms_norm(inputs, norm_gain)
    weights = lax.all_gather(w_qkv, ("gx", "core", "z", "y"), axis=0, tiled=True)
    projected = jnp.dot(normed, weights, preferred_element_type=F32).astype(BF16)
    queries = projected[:, :QW].reshape(rows, KEY_HEADS, REPEATS, HD)

    def absorb(state, keyvals, visible):
        running_max, denominator, numerator = state
        count = keyvals.shape[0]
        key_part = keyvals[:, :KVW].reshape(count, KEY_HEADS, HD)
        value_part = keyvals[:, KVW:].reshape(count, KEY_HEADS, HD)
        scores = jnp.einsum("tgrd,ngd->tgrn", queries, key_part, preferred_element_type=F32) * 0.125
        if visible is not None:
            scores = jnp.where(visible[:, None, None, :], scores, F32(NEG))
        new_max = jnp.maximum(running_max, jnp.max(scores, axis=-1))
        probability = jnp.exp(scores - new_max[..., None])
        if visible is not None:
            probability = jnp.where(visible[:, None, None, :], probability, F32(0.0))
        factor = jnp.exp(running_max - new_max)
        denominator = denominator * factor + jnp.sum(probability, axis=-1)
        numerator = numerator * factor[..., None] + jnp.einsum(
            "tgrn,ngd->tgrd", probability.astype(BF16), value_part, preferred_element_type=F32
        )
        return new_max, denominator, numerator

    def sweep(state, keyvals, key_seg):
        length = min(keyvals.shape[0], 512)

        def step(i, running):
            start = i * length
            part = lax.dynamic_slice_in_dim(keyvals, start, length, 0)
            if key_seg is None:
                return absorb(running, part, None)
            seg_part = lax.dynamic_slice_in_dim(key_seg, start, length, 0)
            key_pos = start + jnp.arange(length, dtype=jnp.int32)
            visible = (seg_part[None, :] == seg_ids[:, None]) & (key_pos[None, :] <= query_pos[:, None])
            return absorb(running, part, visible)

        return lax.fori_loop(0, keyvals.shape[0] // length, step, state)

    query_pos = lax.axis_index(("z", "y")) * rows + jnp.arange(rows, dtype=jnp.int32)
    state = (
        jnp.full((rows, KEY_HEADS, REPEATS), NEG, F32),
        jnp.zeros((rows, KEY_HEADS, REPEATS), F32),
        jnp.zeros((rows, KEY_HEADS, REPEATS, HD), F32),
    )
    along = functools.partial(lax.all_gather, axis_name=("z", "y"), axis=0, tiled=True)
    state = sweep(state, along(prefix_kv[0]), None)
    _, denominator, numerator = sweep(state, along(projected[:, QW:]), along(seg_ids))
    return (numerator / denominator[..., None]).reshape(rows, QW).astype(BF16)[None]


def solution(mesh):
    groups, seqs = mesh.shape["group"], mesh.shape["seq"]
    chips, z_count = groups // 2, seqs // 2
    fine = Mesh(mesh.devices.reshape(chips, 2, z_count, 2), ("gx", "core", "z", "y"))
    group, seq = ("gx", "core"), ("z", "y")
    short = chips == 2 and z_count == SMALL
    return jax.shard_map(
        swap_body if short else gather_body,
        mesh=fine,
        in_specs=(P(group, seq, None), P(), P(group + seq, None), P(group, seq, None), P(group, seq)),
        out_specs=P(group, seq, None),
        check_vma=False,
    )
```

```python
import functools

import jax
import jax.numpy as jnp
from jax import lax
from jax.experimental import pallas as pl
from jax.experimental.pallas import tpu as pltpu
from jax.sharding import Mesh, PartitionSpec as P

HD = 64
QW = 1280
KVW = 320
KEY_HEADS = KVW // HD
REPEATS = QW // KVW
QH = QW // 2
NEG = -1e30
SMALL = 4
PREFIX_WITH_Q = True
CORNER_BY_X = True
Z_ORDER = (1, 2, 3)
WEIGHT = (1, 1, 1, 1)
ORDER = {
    "kv_near_sides": ("kv_z0",),
    "kv_far": ("kv_near_sides", "kv_features", "q_got",),
    "norm": ("kv_near",),
    "q_across": ("kv_far",),
    "normed_pair": ("kv_near_sides",),
    "kv_corner": ("kv_features",),
    "q_line": ("kv_far_sides",),
    "q_res": ("four_back",),
    "prefix_z1": ("kv_far_sides",),
    "prefix_z2": ("q_across",),
    "q_corner": ("two_back",),
    "four_back": ("normed_pair", "prefix_z2",),
    "q_last": ("four_back", "prefix_y",),
    "odd_a": ("prefix_y",),
}
F32 = jnp.float32
BF16 = jnp.bfloat16


def rms_norm(inputs, norm_gain):
    values = inputs.astype(F32)
    mean_square = jnp.mean(values * values, axis=-1, keepdims=True)
    return (values * lax.rsqrt(mean_square + 1e-05) * norm_gain.astype(F32)).astype(BF16)


def swap(x, axis):
    return lax.ppermute(x, axis, [(0, 1), (1, 0)])


def z_swap(x, distance):
    return lax.ppermute(x, "z", [(i, i ^ distance) for i in range(4)])


def sides(piece):
    return swap(piece, "gx"), swap(piece, "y")


def order_kernel(order, bits, *refs):
    sources, out = refs[:-1], refs[-1]
    at = 0
    for source in sources:
        rows, depth = source.shape
        x = source[...]
        for bit in range((depth // 64).bit_length() - 1):
            span = 64 << bit
            parts = [x[:, (i ^ 1) * span:((i ^ 1) + 1) * span] for i in range(depth // span)]
            x = jnp.where(bits[bit] == 1, jnp.concatenate(parts, axis=1), x)
        out[at:at + rows, :] = jnp.concatenate([x[:, b * 64:(b + 1) * 64] for b in order], axis=1)
        at += rows


def order_features(sources, order, bits, weight):
    depth = sources[0].shape[1]
    rows = sum(x.shape[0] for x in sources)
    vmem = pl.BlockSpec(memory_space=pltpu.VMEM)
    return pl.pallas_call(
        functools.partial(order_kernel, order),
        out_shape=jax.ShapeDtypeStruct((rows, 64 * len(order)), BF16),
        in_specs=[pl.BlockSpec(memory_space=pltpu.SMEM)] + [vmem] * len(sources),
        out_specs=vmem,
        compiler_params=pltpu.CompilerParams(vmem_limit_bytes=24 << 20),
        cost_estimate=pl.CostEstimate(flops=0, bytes_accessed=weight * 4 * rows * depth, transcendentals=0),
    )(bits, *sources)


def add_products(total, features, at, pieces):
    for piece in pieces:
        rows = piece.shape[0]
        term = jnp.dot(features[:, at:at + rows], piece[...], preferred_element_type=F32)
        total = term if total is None else total + term
        at += rows
    return total


def first_kernel(features, *refs):
    pieces, out = refs[:-1], refs[-1]
    out[...] = add_products(None, features, 0, pieces)


def last_kernel(at, keep, features, so_far, *refs):
    pieces, (kept, sent) = refs[:-2], refs[-2:]
    total = add_products(so_far[...], features, at, pieces)
    rows = total.shape[0] // (2 * keep)
    for i in range(keep):
        kept[i * rows:(i + 1) * rows, :] = total[2 * i * rows:(2 * i + 1) * rows]
        sent[i * rows:(i + 1) * rows, :] = total[(2 * i + 1) * rows:(2 * i + 2) * rows]


def project(features, pieces, late, keep, weight):
    rows, depth = features.shape
    width = pieces[0].shape[1]
    vmem = pl.BlockSpec(memory_space=pltpu.VMEM)
    early = len(pieces) - late
    params = pltpu.CompilerParams(vmem_limit_bytes=24 << 20)
    done = sum(p.shape[0] for p in pieces[:early])

    def cost(deep):
        return pl.CostEstimate(flops=2 * rows * deep * width, bytes_accessed=2 * deep * (width + rows), transcendentals=0)

    so_far = pl.pallas_call(
        first_kernel,
        out_shape=jax.ShapeDtypeStruct((rows, width), F32),
        in_specs=[vmem] * (1 + early),
        out_specs=vmem,
        compiler_params=params,
        cost_estimate=cost(weight * done),
    )(features, *pieces[:early])
    return pl.pallas_call(
        functools.partial(last_kernel, done, keep),
        out_shape=[jax.ShapeDtypeStruct((rows // 2, width), F32)] * 2,
        in_specs=[vmem] * (2 + late),
        out_specs=[vmem, vmem],
        compiler_params=params,
        cost_estimate=cost(depth - done),
    )(features, so_far, *pieces[early:])


def after(first, *then):
    return lax.optimization_barrier((first,) + then)[1:]


def attend_kernel(earlier, scalars, mine, pair, prefix, seg_col, *refs):
    blocks, out, q_all = refs[:earlier + 1], refs[earlier + 1], refs[earlier + 2]
    half = scalars[0]
    rows = mine.shape[0]
    q_all[half] = mine[...]
    q_all[1 - half] = pair[...]
    biases = []
    q_seg = seg_col[...]
    for i, block in enumerate(blocks):
        k_seg = block[rows:rows + 1, :rows].astype(F32)
        seen = q_seg == k_seg
        if i == 0:
            q_at = lax.broadcasted_iota(jnp.int32, (rows, rows), 0)
            k_at = lax.broadcasted_iota(jnp.int32, (rows, rows), 1)
            seen = seen & (k_at <= q_at)
            biases.append(jnp.where(seen, 0.0, NEG))
        else:
            biases.append(jnp.where(seen, jnp.where(scalars[1 + i] == 0, 0.0, NEG), NEG))
    bias = jnp.concatenate(biases, axis=1)
    bias = jnp.concatenate([bias] * REPEATS, axis=0)
    for head in range(KEY_HEADS):
        cols, vcols = slice(head * HD, (head + 1) * HD), slice(KVW + head * HD, KVW + (head + 1) * HD)
        base = head * REPEATS * HD
        heads = [divmod(head * REPEATS + r, QH // HD) for r in range(REPEATS)]
        queries = jnp.concatenate([q_all[part, :, h * HD:(h + 1) * HD] for part, h in heads], axis=0)
        keys = jnp.concatenate([block[:rows, cols] for block in blocks], axis=0)
        values = jnp.concatenate([block[:rows, vcols] for block in blocks], axis=0)
        contract = (((1,), (1,)), ((), ()))
        s_pre = lax.dot_general(queries, prefix[:, cols], contract, preferred_element_type=F32)
        s_suf = lax.dot_general(queries, keys, contract, preferred_element_type=F32) + bias
        top = jnp.maximum(jnp.max(s_pre, axis=-1, keepdims=True), jnp.max(s_suf, axis=-1, keepdims=True))
        p_pre, p_suf = jnp.exp(s_pre - top), jnp.exp(s_suf - top)
        total = jnp.sum(p_pre, axis=-1, keepdims=True) + jnp.sum(p_suf, axis=-1, keepdims=True)
        numerator = jnp.dot(p_pre.astype(BF16), prefix[:, vcols], preferred_element_type=F32)
        numerator += jnp.dot(p_suf.astype(BF16), values, preferred_element_type=F32)
        context = (numerator / total).astype(BF16)
        for r in range(REPEATS):
            out[:, base + r * HD:base + (r + 1) * HD] = context[r * rows:(r + 1) * rows]


def attend(halves, prefix, seg_col, blocks, scalars):
    rows = halves[0].shape[0]
    earlier = len(blocks) - 1
    vmem = pl.BlockSpec(memory_space=pltpu.VMEM)
    keys = prefix.shape[0] + rows * (earlier + 1)
    return pl.pallas_call(
        functools.partial(attend_kernel, earlier),
        out_shape=jax.ShapeDtypeStruct((rows, QW), BF16),
        in_specs=[pl.BlockSpec(memory_space=pltpu.SMEM)] + [vmem] * (4 + len(blocks)),
        out_specs=vmem,
        scratch_shapes=[pltpu.VMEM((2, rows, QH), BF16)],
        compiler_params=pltpu.CompilerParams(vmem_limit_bytes=40 << 20),
        cost_estimate=pl.CostEstimate(
            flops=4 * rows * keys * QW, bytes_accessed=4 * keys * KVW, transcendentals=rows * keys * QW // HD
        ),
    )(scalars, *halves, prefix, seg_col, *blocks)


def swap_body(tokens, norm_gain, w_qkv, prefix_kv, segments):
    inputs, seg_ids, own_prefix = tokens[0], segments[0], prefix_kv[0]
    rows = inputs.shape[0]
    gx, core, z, y = (lax.axis_index(a) for a in ("gx", "core", "z", "y"))
    z_count, y_count = lax.axis_size("z"), lax.axis_size("y")
    index = z * y_count + y
    depth = w_qkv.shape[0]

    have = {}

    def gate(point, *values):
        names = [n for n in ORDER.get(point, ()) if n in have]
        return after(tuple(have[n] for n in names), *values) if names else values

    kv_near = w_qkv[:, QW:]
    kv_zs = []
    for d in Z_ORDER:
        kv_zs.append(z_swap(*gate(f"kv_z{len(kv_zs)}", kv_near), d))
        have[f"kv_z{len(kv_zs) - 1}"] = kv_zs[-1]
    kv_near_sides = sides(*gate("kv_near_sides", kv_near))
    have["kv_near_sides"] = kv_near_sides

    pair = z & 1
    (w_own,) = gate("q_rows", w_qkv)
    q_got = z_swap(
        jnp.concatenate(
            [lax.dynamic_slice_in_dim(w_own, (1 - pair) * QH, QH, 1)] + ([own_prefix] if PREFIX_WITH_Q else [])
        ),
        1,
    )
    have["q_got"] = q_got
    q_near = jnp.concatenate([lax.dynamic_slice_in_dim(w_own, pair * QH, QH, 1), q_got[:depth]])

    kv_far = jnp.concatenate(gate("kv_far", *kv_zs))
    have["kv_far"] = kv_far
    kv_far_sides = sides(kv_far)
    have["kv_far_sides"] = kv_far_sides

    (normed_in,) = gate("norm", inputs)
    normed = rms_norm(normed_in, norm_gain)
    normed_sibling = swap(normed, "core")
    have["normed_sibling"] = normed_sibling
    number = ((gx * 2 + core) * z_count + z) * y_count + y
    bits = jnp.stack([(number >> i) & 1 for i in range(5)]).astype(jnp.int32)
    zs = (0,) + tuple(Z_ORDER)

    def blocks_at(dx, dy, dzs):
        return [(dx * 8 + dz) * 2 + dy for dz in dzs]

    kv_order = []
    for dx, dy, dzs in (
        (0, 0, zs[:1]), (1, 0, zs[:1]), (0, 1, zs[:1]), (0, 0, zs[1:]), (1, 0, zs[1:]), (0, 1, zs[1:]), (1, 1, zs)
    ):
        kv_order += blocks_at(dx, dy, dzs)
    kv_features = order_features([normed, normed_sibling], kv_order, bits, WEIGHT[0])
    have["kv_features"] = kv_features

    (q_load,) = gate("q_across", q_near)
    if PREFIX_WITH_Q:
        q_load = jnp.concatenate([q_load, own_prefix, q_got[depth:]])
    q_across = z_swap(q_load, 2)
    have["q_across"] = q_across
    normed_pair = z_swap(*gate("normed_pair", normed), 1)
    have["normed_pair"] = normed_pair

    near_x, far_x, far_y = gate("kv_corner", kv_near_sides[0], *kv_far_sides)
    kv_low = swap(jnp.concatenate([near_x, far_x[:depth]]), "y")
    kv_high = swap(far_y[depth:], "gx")
    have["kv_corner"] = (kv_low, kv_high)
    if not PREFIX_WITH_Q:
        (line,) = gate("prefix_z1", own_prefix)
        line = jnp.concatenate([line, z_swap(line, 1)])
        have["prefix_z1"] = line
    kv_pieces = [kv_near, *kv_near_sides, kv_far, *kv_far_sides, *gate("kv_last", kv_low, kv_high)]
    kv_kept, kv_sent = project(kv_features, kv_pieces, 2, 1, WEIGHT[2])
    have["kv_theirs"] = kv_sent
    kv_other = swap(*gate("kv_other", kv_sent), "core")
    have["kv_other"] = kv_other
    q_line = jnp.concatenate([q_near, *gate("q_line", q_across[:2 * depth])])
    q_line_x, q_line_y = sides(q_line)
    have["q_sides"] = (q_line_x, q_line_y)
    seg_row = jnp.pad(seg_ids.astype(BF16)[None, :], ((0, 7), (0, 2 * KVW - rows)))
    block = jnp.concatenate([(kv_kept + kv_other).astype(BF16), seg_row], axis=0)
    have["block"] = block
    if PREFIX_WITH_Q:
        line = jnp.concatenate([own_prefix, q_got[depth:], q_across[2 * depth:]])
    else:
        (line,) = gate("prefix_z2", line)
        line = jnp.concatenate([line, z_swap(line, 2)])
    have["prefix_z2"] = line

    upward = [(i, i + 1) for i in range(z_count - 1)]
    two_back = lax.ppermute(*gate("two_back", block), "z", upward)
    have["two_back"] = two_back
    prefix = jnp.concatenate([line, swap(*gate("prefix_y", line), "y")])
    have["prefix_y"] = prefix
    four_back = lax.ppermute(*gate("four_back", two_back), "z", upward)
    have["four_back"] = four_back
    odd_a = swap(*gate("odd_a", two_back), "y")
    have["odd_a"] = odd_a

    q_late_x, q_late_y = gate("q_corner", q_line_x, q_line_y)
    if CORNER_BY_X:
        q_corners = [swap(q_late_y, "gx")]
    else:
        q_corners = [swap(q_late_x[:2 * depth], "y"), swap(q_late_y[2 * depth:], "gx")]
    have["q_corner"] = q_corners
    odd_b = swap(*gate("odd_b", jnp.where(y == 0, block, four_back)), "y")
    have["odd_b"] = odd_b
    blocks = [block, two_back, four_back, odd_a, odd_b]
    distances = [0, 2, 4, 1 + 2 * y, 3 - 2 * y]

    q_pieces = [q_line, q_line_x, q_line_y, *gate("q_last", *q_corners)]
    q_order = []
    for dx, dy in ((0, 0), (1, 0), (0, 1), (1, 1)):
        q_order += blocks_at(dx, dy, (0, 1, 2, 3))
    (normed_pair,) = gate("diagonal", normed_pair)
    normed_diagonal = swap(normed_pair, "core")
    q_features = order_features([normed, normed_sibling, normed_pair, normed_diagonal], q_order, bits, WEIGHT[1])
    q_kept, q_sent = project(q_features, q_pieces, len(q_corners), 2, WEIGHT[3])
    queries = (q_kept + swap(q_sent, "core")).astype(BF16) * jnp.asarray(0.125, BF16)
    halves = [queries[:rows], z_swap(*gate("q_res", queries[rows:]), 1)]

    scalars = jnp.stack([pair] + [jnp.where(index >= d, 0, 1) for d in distances]).astype(jnp.int32)
    context = attend(halves, prefix, seg_ids.astype(F32)[:, None], blocks, scalars)
    return context[None]


def gather_body(tokens, norm_gain, w_qkv, prefix_kv, segments):
    inputs, seg_ids = tokens[0], segments[0]
    rows = inputs.shape[0]
    normed = rms_norm(inputs, norm_gain)
    weights = lax.all_gather(w_qkv, ("gx", "core", "z", "y"), axis=0, tiled=True)
    projected = jnp.dot(normed, weights, preferred_element_type=F32).astype(BF16)
    queries = projected[:, :QW].reshape(rows, KEY_HEADS, REPEATS, HD)

    def absorb(state, keyvals, visible):
        running_max, denominator, numerator = state
        count = keyvals.shape[0]
        key_part = keyvals[:, :KVW].reshape(count, KEY_HEADS, HD)
        value_part = keyvals[:, KVW:].reshape(count, KEY_HEADS, HD)
        scores = jnp.einsum("tgrd,ngd->tgrn", queries, key_part, preferred_element_type=F32) * 0.125
        if visible is not None:
            scores = jnp.where(visible[:, None, None, :], scores, F32(NEG))
        new_max = jnp.maximum(running_max, jnp.max(scores, axis=-1))
        probability = jnp.exp(scores - new_max[..., None])
        if visible is not None:
            probability = jnp.where(visible[:, None, None, :], probability, F32(0.0))
        factor = jnp.exp(running_max - new_max)
        denominator = denominator * factor + jnp.sum(probability, axis=-1)
        numerator = numerator * factor[..., None] + jnp.einsum(
            "tgrn,ngd->tgrd", probability.astype(BF16), value_part, preferred_element_type=F32
        )
        return new_max, denominator, numerator

    def sweep(state, keyvals, key_seg):
        length = min(keyvals.shape[0], 512)

        def step(i, running):
            start = i * length
            part = lax.dynamic_slice_in_dim(keyvals, start, length, 0)
            if key_seg is None:
                return absorb(running, part, None)
            seg_part = lax.dynamic_slice_in_dim(key_seg, start, length, 0)
            key_pos = start + jnp.arange(length, dtype=jnp.int32)
            visible = (seg_part[None, :] == seg_ids[:, None]) & (key_pos[None, :] <= query_pos[:, None])
            return absorb(running, part, visible)

        return lax.fori_loop(0, keyvals.shape[0] // length, step, state)

    query_pos = lax.axis_index(("z", "y")) * rows + jnp.arange(rows, dtype=jnp.int32)
    state = (
        jnp.full((rows, KEY_HEADS, REPEATS), NEG, F32),
        jnp.zeros((rows, KEY_HEADS, REPEATS), F32),
        jnp.zeros((rows, KEY_HEADS, REPEATS, HD), F32),
    )
    along = functools.partial(lax.all_gather, axis_name=("z", "y"), axis=0, tiled=True)
    state = sweep(state, along(prefix_kv[0]), None)
    _, denominator, numerator = sweep(state, along(projected[:, QW:]), along(seg_ids))
    return (numerator / denominator[..., None]).reshape(rows, QW).astype(BF16)[None]


def solution(mesh):
    groups, seqs = mesh.shape["group"], mesh.shape["seq"]
    chips, z_count = groups // 2, seqs // 2
    fine = Mesh(mesh.devices.reshape(chips, 2, z_count, 2), ("gx", "core", "z", "y"))
    group, seq = ("gx", "core"), ("z", "y")
    short = chips == 2 and z_count == SMALL
    return jax.shard_map(
        swap_body if short else gather_body,
        mesh=fine,
        in_specs=(P(group, seq, None), P(), P(group + seq, None), P(group, seq, None), P(group, seq)),
        out_specs=P(group, seq, None),
        check_vma=False,
    )
```

```python
import functools

import jax
import jax.numpy as jnp
from jax import lax
from jax.experimental import pallas as pl
from jax.experimental.pallas import tpu as pltpu
from jax.sharding import Mesh, PartitionSpec as P

HD = 64
QW = 1280
KVW = 320
KEY_HEADS = KVW // HD
REPEATS = QW // KVW
QH = QW // 2
NEG = -1e30
SMALL = 4
PREFIX_WITH_Q = 2
CORNER_BY_X = True
Z_ORDER = (1, 2, 3)
WEIGHT = (1, 1, 1, 1)
ORDER = {
    "kv_near_sides": ("kv_z0",),
    "kv_far": ("kv_near_sides", "kv_features", "q_got",),
    "norm": ("kv_near",),
    "q_across": ("kv_far",),
    "normed_pair": ("kv_near_sides",),
    "kv_corner": ("kv_features",),
    "q_line": ("kv_far_sides",),
    "q_res": ("four_back",),
    "prefix_z1": ("kv_far_sides",),
    "prefix_z2": ("q_across",),
    "q_corner": ("two_back",),
    "four_back": ("normed_pair", "prefix_z2", "q_features",),
    "q_last": ("four_back", "prefix_y", "odd_a",),
}
F32 = jnp.float32
BF16 = jnp.bfloat16


def rms_norm(inputs, norm_gain):
    values = inputs.astype(F32)
    mean_square = jnp.mean(values * values, axis=-1, keepdims=True)
    return (values * lax.rsqrt(mean_square + 1e-05) * norm_gain.astype(F32)).astype(BF16)


def swap(x, axis):
    return lax.ppermute(x, axis, [(0, 1), (1, 0)])


def z_swap(x, distance):
    return lax.ppermute(x, "z", [(i, i ^ distance) for i in range(4)])


def sides(piece):
    return swap(piece, "gx"), swap(piece, "y")


def order_kernel(order, bits, *refs):
    sources, out = refs[:-1], refs[-1]
    at = 0
    for source in sources:
        rows, depth = source.shape
        x = source[...]
        for bit in range((depth // 64).bit_length() - 1):
            span = 64 << bit
            parts = [x[:, (i ^ 1) * span:((i ^ 1) + 1) * span] for i in range(depth // span)]
            x = jnp.where(bits[bit] == 1, jnp.concatenate(parts, axis=1), x)
        out[at:at + rows, :] = jnp.concatenate([x[:, b * 64:(b + 1) * 64] for b in order], axis=1)
        at += rows


def order_features(sources, order, bits, weight):
    depth = sources[0].shape[1]
    rows = sum(x.shape[0] for x in sources)
    vmem = pl.BlockSpec(memory_space=pltpu.VMEM)
    return pl.pallas_call(
        functools.partial(order_kernel, order),
        out_shape=jax.ShapeDtypeStruct((rows, 64 * len(order)), BF16),
        in_specs=[pl.BlockSpec(memory_space=pltpu.SMEM)] + [vmem] * len(sources),
        out_specs=vmem,
        compiler_params=pltpu.CompilerParams(vmem_limit_bytes=24 << 20),
        cost_estimate=pl.CostEstimate(flops=0, bytes_accessed=weight * 4 * rows * depth, transcendentals=0),
    )(bits, *sources)


def add_products(total, features, at, pieces):
    for piece in pieces:
        rows = piece.shape[0]
        term = jnp.dot(features[:, at:at + rows], piece[...], preferred_element_type=F32)
        total = term if total is None else total + term
        at += rows
    return total


def first_kernel(features, *refs):
    pieces, out = refs[:-1], refs[-1]
    out[...] = add_products(None, features, 0, pieces)


def last_kernel(at, keep, features, so_far, *refs):
    pieces, (kept, sent) = refs[:-2], refs[-2:]
    total = add_products(so_far[...], features, at, pieces)
    rows = total.shape[0] // (2 * keep)
    for i in range(keep):
        kept[i * rows:(i + 1) * rows, :] = total[2 * i * rows:(2 * i + 1) * rows]
        sent[i * rows:(i + 1) * rows, :] = total[(2 * i + 1) * rows:(2 * i + 2) * rows]


def project(features, pieces, late, keep, weight):
    rows, depth = features.shape
    width = pieces[0].shape[1]
    vmem = pl.BlockSpec(memory_space=pltpu.VMEM)
    early = len(pieces) - late
    params = pltpu.CompilerParams(vmem_limit_bytes=24 << 20)
    done = sum(p.shape[0] for p in pieces[:early])

    def cost(deep):
        return pl.CostEstimate(flops=2 * rows * deep * width, bytes_accessed=2 * deep * (width + rows), transcendentals=0)

    so_far = pl.pallas_call(
        first_kernel,
        out_shape=jax.ShapeDtypeStruct((rows, width), F32),
        in_specs=[vmem] * (1 + early),
        out_specs=vmem,
        compiler_params=params,
        cost_estimate=cost(weight * done),
    )(features, *pieces[:early])
    return pl.pallas_call(
        functools.partial(last_kernel, done, keep),
        out_shape=[jax.ShapeDtypeStruct((rows // 2, width), F32)] * 2,
        in_specs=[vmem] * (2 + late),
        out_specs=[vmem, vmem],
        compiler_params=params,
        cost_estimate=cost(depth - done),
    )(features, so_far, *pieces[early:])


def after(first, *then):
    return lax.optimization_barrier((first,) + then)[1:]


def attend_kernel(earlier, scalars, mine, pair, prefix, seg_col, *refs):
    blocks, out, q_all = refs[:earlier + 1], refs[earlier + 1], refs[earlier + 2]
    half = scalars[0]
    rows = mine.shape[0]
    q_all[half] = mine[...]
    q_all[1 - half] = pair[...]
    biases = []
    q_seg = seg_col[...]
    for i, block in enumerate(blocks):
        k_seg = block[rows:rows + 1, :rows].astype(F32)
        seen = q_seg == k_seg
        if i == 0:
            q_at = lax.broadcasted_iota(jnp.int32, (rows, rows), 0)
            k_at = lax.broadcasted_iota(jnp.int32, (rows, rows), 1)
            seen = seen & (k_at <= q_at)
            biases.append(jnp.where(seen, 0.0, NEG))
        else:
            biases.append(jnp.where(seen, jnp.where(scalars[1 + i] == 0, 0.0, NEG), NEG))
    bias = jnp.concatenate(biases, axis=1)
    bias = jnp.concatenate([bias] * REPEATS, axis=0)
    for head in range(KEY_HEADS):
        cols, vcols = slice(head * HD, (head + 1) * HD), slice(KVW + head * HD, KVW + (head + 1) * HD)
        base = head * REPEATS * HD
        heads = [divmod(head * REPEATS + r, QH // HD) for r in range(REPEATS)]
        queries = jnp.concatenate([q_all[part, :, h * HD:(h + 1) * HD] for part, h in heads], axis=0)
        keys = jnp.concatenate([block[:rows, cols] for block in blocks], axis=0)
        values = jnp.concatenate([block[:rows, vcols] for block in blocks], axis=0)
        contract = (((1,), (1,)), ((), ()))
        s_pre = lax.dot_general(queries, prefix[:, cols], contract, preferred_element_type=F32)
        s_suf = lax.dot_general(queries, keys, contract, preferred_element_type=F32) + bias
        top = jnp.maximum(jnp.max(s_pre, axis=-1, keepdims=True), jnp.max(s_suf, axis=-1, keepdims=True))
        p_pre, p_suf = jnp.exp(s_pre - top), jnp.exp(s_suf - top)
        total = jnp.sum(p_pre, axis=-1, keepdims=True) + jnp.sum(p_suf, axis=-1, keepdims=True)
        numerator = jnp.dot(p_pre.astype(BF16), prefix[:, vcols], preferred_element_type=F32)
        numerator += jnp.dot(p_suf.astype(BF16), values, preferred_element_type=F32)
        context = (numerator / total).astype(BF16)
        for r in range(REPEATS):
            out[:, base + r * HD:base + (r + 1) * HD] = context[r * rows:(r + 1) * rows]


def attend(halves, prefix, seg_col, blocks, scalars):
    rows = halves[0].shape[0]
    earlier = len(blocks) - 1
    vmem = pl.BlockSpec(memory_space=pltpu.VMEM)
    keys = prefix.shape[0] + rows * (earlier + 1)
    return pl.pallas_call(
        functools.partial(attend_kernel, earlier),
        out_shape=jax.ShapeDtypeStruct((rows, QW), BF16),
        in_specs=[pl.BlockSpec(memory_space=pltpu.SMEM)] + [vmem] * (4 + len(blocks)),
        out_specs=vmem,
        scratch_shapes=[pltpu.VMEM((2, rows, QH), BF16)],
        compiler_params=pltpu.CompilerParams(vmem_limit_bytes=40 << 20),
        cost_estimate=pl.CostEstimate(
            flops=4 * rows * keys * QW, bytes_accessed=4 * keys * KVW, transcendentals=rows * keys * QW // HD
        ),
    )(scalars, *halves, prefix, seg_col, *blocks)


def swap_body(tokens, norm_gain, w_qkv, prefix_kv, segments):
    inputs, seg_ids, own_prefix = tokens[0], segments[0], prefix_kv[0]
    rows = inputs.shape[0]
    gx, core, z, y = (lax.axis_index(a) for a in ("gx", "core", "z", "y"))
    z_count, y_count = lax.axis_size("z"), lax.axis_size("y")
    index = z * y_count + y
    depth = w_qkv.shape[0]

    have = {}

    def gate(point, *values):
        names = [n for n in ORDER.get(point, ()) if n in have]
        return after(tuple(have[n] for n in names), *values) if names else values

    kv_near = w_qkv[:, QW:]
    kv_zs = []
    for d in Z_ORDER:
        kv_zs.append(z_swap(*gate(f"kv_z{len(kv_zs)}", kv_near), d))
        have[f"kv_z{len(kv_zs) - 1}"] = kv_zs[-1]
    kv_near_sides = sides(*gate("kv_near_sides", kv_near))
    have["kv_near_sides"] = kv_near_sides

    pair = z & 1
    (w_own,) = gate("q_rows", w_qkv)
    q_got = z_swap(
        jnp.concatenate(
            [lax.dynamic_slice_in_dim(w_own, (1 - pair) * QH, QH, 1)] + ([own_prefix] if PREFIX_WITH_Q else [])
        ),
        1,
    )
    have["q_got"] = q_got
    q_near = jnp.concatenate([lax.dynamic_slice_in_dim(w_own, pair * QH, QH, 1), q_got[:depth]])

    kv_far = jnp.concatenate(gate("kv_far", *kv_zs))
    have["kv_far"] = kv_far
    kv_far_sides = sides(kv_far)
    have["kv_far_sides"] = kv_far_sides

    (normed_in,) = gate("norm", inputs)
    normed = rms_norm(normed_in, norm_gain)
    normed_sibling = swap(normed, "core")
    have["normed_sibling"] = normed_sibling
    number = ((gx * 2 + core) * z_count + z) * y_count + y
    bits = jnp.stack([(number >> i) & 1 for i in range(5)]).astype(jnp.int32)
    zs = (0,) + tuple(Z_ORDER)

    def blocks_at(dx, dy, dzs):
        return [(dx * 8 + dz) * 2 + dy for dz in dzs]

    kv_order = []
    for dx, dy, dzs in (
        (0, 0, zs[:1]), (1, 0, zs[:1]), (0, 1, zs[:1]), (0, 0, zs[1:]), (1, 0, zs[1:]), (0, 1, zs[1:]), (1, 1, zs)
    ):
        kv_order += blocks_at(dx, dy, dzs)
    kv_features = order_features([normed, normed_sibling], kv_order, bits, WEIGHT[0])
    have["kv_features"] = kv_features

    (q_load,) = gate("q_across", q_near)
    if PREFIX_WITH_Q == 1:
        q_load = jnp.concatenate([q_load, own_prefix, q_got[depth:]])
    q_across = z_swap(q_load, 2)
    have["q_across"] = q_across
    normed_pair = z_swap(*gate("normed_pair", normed), 1)
    have["normed_pair"] = normed_pair

    near_x, far_x, far_y = gate("kv_corner", kv_near_sides[0], *kv_far_sides)
    kv_low = swap(jnp.concatenate([near_x, far_x[:depth]]), "y")
    kv_high = swap(far_y[depth:], "gx")
    have["kv_corner"] = (kv_low, kv_high)
    if not PREFIX_WITH_Q:
        (line,) = gate("prefix_z1", own_prefix)
        line = jnp.concatenate([line, z_swap(line, 1)])
        have["prefix_z1"] = line
    kv_pieces = [kv_near, *kv_near_sides, kv_far, *kv_far_sides, *gate("kv_last", kv_low, kv_high)]
    kv_kept, kv_sent = project(kv_features, kv_pieces, 2, 1, WEIGHT[2])
    have["kv_theirs"] = kv_sent
    kv_other = swap(*gate("kv_other", kv_sent), "core")
    have["kv_other"] = kv_other
    q_line = jnp.concatenate([q_near, *gate("q_line", q_across[:2 * depth])])
    q_line_x, q_line_y = sides(q_line)
    have["q_sides"] = (q_line_x, q_line_y)
    seg_row = jnp.pad(seg_ids.astype(BF16)[None, :], ((0, 7), (0, 2 * KVW - rows)))
    block = jnp.concatenate([(kv_kept + kv_other).astype(BF16), seg_row], axis=0)
    have["block"] = block
    if PREFIX_WITH_Q == 1:
        line = jnp.concatenate([own_prefix, q_got[depth:], q_across[2 * depth:]])
    else:
        if PREFIX_WITH_Q:
            line = jnp.concatenate([own_prefix, q_got[depth:]])
        (line,) = gate("prefix_z2", line)
        line = jnp.concatenate([line, z_swap(line, 2)])
    have["prefix_z2"] = line

    q_order = []
    for dx, dy in ((0, 0), (1, 0), (0, 1), (1, 1)):
        q_order += blocks_at(dx, dy, (0, 1, 2, 3))
    (normed_pair,) = gate("diagonal", normed_pair)
    normed_diagonal = swap(normed_pair, "core")
    q_features = order_features([normed, normed_sibling, normed_pair, normed_diagonal], q_order, bits, WEIGHT[1])
    have["q_features"] = q_features

    upward = [(i, i + 1) for i in range(z_count - 1)]
    two_back = lax.ppermute(*gate("two_back", block), "z", upward)
    have["two_back"] = two_back
    prefix = jnp.concatenate([line, swap(*gate("prefix_y", line), "y")])
    have["prefix_y"] = prefix
    four_back = lax.ppermute(*gate("four_back", two_back), "z", upward)
    have["four_back"] = four_back
    odd_a = swap(*gate("odd_a", two_back), "y")
    have["odd_a"] = odd_a

    q_late_x, q_late_y = gate("q_corner", q_line_x, q_line_y)
    if CORNER_BY_X:
        q_corners = [swap(q_late_y, "gx")]
    else:
        q_corners = [swap(q_late_x[:2 * depth], "y"), swap(q_late_y[2 * depth:], "gx")]
    have["q_corner"] = q_corners
    odd_b = swap(*gate("odd_b", jnp.where(y == 0, block, four_back)), "y")
    have["odd_b"] = odd_b
    blocks = [block, two_back, four_back, odd_a, odd_b]
    distances = [0, 2, 4, 1 + 2 * y, 3 - 2 * y]

    q_pieces = [q_line, q_line_x, q_line_y, *gate("q_last", *q_corners)]
    q_kept, q_sent = project(q_features, q_pieces, len(q_corners), 2, WEIGHT[3])
    queries = (q_kept + swap(q_sent, "core")).astype(BF16) * jnp.asarray(0.125, BF16)
    halves = [queries[:rows], z_swap(*gate("q_res", queries[rows:]), 1)]

    scalars = jnp.stack([pair] + [jnp.where(index >= d, 0, 1) for d in distances]).astype(jnp.int32)
    context = attend(halves, prefix, seg_ids.astype(F32)[:, None], blocks, scalars)
    return context[None]


def gather_body(tokens, norm_gain, w_qkv, prefix_kv, segments):
    inputs, seg_ids = tokens[0], segments[0]
    rows = inputs.shape[0]
    normed = rms_norm(inputs, norm_gain)
    weights = lax.all_gather(w_qkv, ("gx", "core", "z", "y"), axis=0, tiled=True)
    projected = jnp.dot(normed, weights, preferred_element_type=F32).astype(BF16)
    queries = projected[:, :QW].reshape(rows, KEY_HEADS, REPEATS, HD)

    def absorb(state, keyvals, visible):
        running_max, denominator, numerator = state
        count = keyvals.shape[0]
        key_part = keyvals[:, :KVW].reshape(count, KEY_HEADS, HD)
        value_part = keyvals[:, KVW:].reshape(count, KEY_HEADS, HD)
        scores = jnp.einsum("tgrd,ngd->tgrn", queries, key_part, preferred_element_type=F32) * 0.125
        if visible is not None:
            scores = jnp.where(visible[:, None, None, :], scores, F32(NEG))
        new_max = jnp.maximum(running_max, jnp.max(scores, axis=-1))
        probability = jnp.exp(scores - new_max[..., None])
        if visible is not None:
            probability = jnp.where(visible[:, None, None, :], probability, F32(0.0))
        factor = jnp.exp(running_max - new_max)
        denominator = denominator * factor + jnp.sum(probability, axis=-1)
        numerator = numerator * factor[..., None] + jnp.einsum(
            "tgrn,ngd->tgrd", probability.astype(BF16), value_part, preferred_element_type=F32
        )
        return new_max, denominator, numerator

    def sweep(state, keyvals, key_seg):
        length = min(keyvals.shape[0], 512)

        def step(i, running):
            start = i * length
            part = lax.dynamic_slice_in_dim(keyvals, start, length, 0)
            if key_seg is None:
                return absorb(running, part, None)
            seg_part = lax.dynamic_slice_in_dim(key_seg, start, length, 0)
            key_pos = start + jnp.arange(length, dtype=jnp.int32)
            visible = (seg_part[None, :] == seg_ids[:, None]) & (key_pos[None, :] <= query_pos[:, None])
            return absorb(running, part, visible)

        return lax.fori_loop(0, keyvals.shape[0] // length, step, state)

    query_pos = lax.axis_index(("z", "y")) * rows + jnp.arange(rows, dtype=jnp.int32)
    state = (
        jnp.full((rows, KEY_HEADS, REPEATS), NEG, F32),
        jnp.zeros((rows, KEY_HEADS, REPEATS), F32),
        jnp.zeros((rows, KEY_HEADS, REPEATS, HD), F32),
    )
    along = functools.partial(lax.all_gather, axis_name=("z", "y"), axis=0, tiled=True)
    state = sweep(state, along(prefix_kv[0]), None)
    _, denominator, numerator = sweep(state, along(projected[:, QW:]), along(seg_ids))
    return (numerator / denominator[..., None]).reshape(rows, QW).astype(BF16)[None]


def solution(mesh):
    groups, seqs = mesh.shape["group"], mesh.shape["seq"]
    chips, z_count = groups // 2, seqs // 2
    fine = Mesh(mesh.devices.reshape(chips, 2, z_count, 2), ("gx", "core", "z", "y"))
    group, seq = ("gx", "core"), ("z", "y")
    short = chips == 2 and z_count == SMALL
    return jax.shard_map(
        swap_body if short else gather_body,
        mesh=fine,
        in_specs=(P(group, seq, None), P(), P(group + seq, None), P(group, seq, None), P(group, seq)),
        out_specs=P(group, seq, None),
        check_vma=False,
    )
```

```python
import functools

import jax
import jax.numpy as jnp
from jax import lax
from jax.experimental import pallas as pl
from jax.experimental.pallas import tpu as pltpu
from jax.sharding import Mesh, PartitionSpec as P

HD = 64
QW = 1280
KVW = 320
KEY_HEADS = KVW // HD
REPEATS = QW // KVW
QH = QW // 2
NEG = -1e30
SMALL = 4
PREFIX_WITH_Q = 2
CORNER_BY_X = True
Z_ORDER = (1, 2, 3)
WEIGHT = (1, 1, 1, 1)
ORDER = {
    "kv_near_sides": ("kv_z0",),
    "kv_far": ("kv_near_sides", "kv_features", "q_got",),
    "q_across": ("kv_far",),
    "normed_pair": ("kv_near_sides",),
    "kv_corner": ("kv_features",),
    "q_line": ("kv_far_sides",),
    "q_res": ("four_back", "odd_a",),
    "prefix_z1": ("kv_far_sides",),
    "prefix_z2": ("q_across",),
    "q_corner": ("two_back",),
    "four_back": ("normed_pair", "prefix_z2", "q_features",),
    "q_last": ("four_back", "prefix_y", "odd_a",),
}
F32 = jnp.float32
BF16 = jnp.bfloat16


def rms_norm(inputs, norm_gain):
    values = inputs.astype(F32)
    mean_square = jnp.mean(values * values, axis=-1, keepdims=True)
    return (values * lax.rsqrt(mean_square + 1e-05) * norm_gain.astype(F32)).astype(BF16)


def swap(x, axis):
    return lax.ppermute(x, axis, [(0, 1), (1, 0)])


def z_swap(x, distance):
    return lax.ppermute(x, "z", [(i, i ^ distance) for i in range(4)])


def sides(piece):
    return swap(piece, "gx"), swap(piece, "y")


def order_kernel(order, bits, *refs):
    sources, out = refs[:-1], refs[-1]
    at = 0
    for source in sources:
        rows, depth = source.shape
        x = source[...]
        for bit in range((depth // 64).bit_length() - 1):
            span = 64 << bit
            parts = [x[:, (i ^ 1) * span:((i ^ 1) + 1) * span] for i in range(depth // span)]
            x = jnp.where(bits[bit] == 1, jnp.concatenate(parts, axis=1), x)
        out[at:at + rows, :] = jnp.concatenate([x[:, b * 64:(b + 1) * 64] for b in order], axis=1)
        at += rows


def order_features(sources, order, bits, weight):
    depth = sources[0].shape[1]
    rows = sum(x.shape[0] for x in sources)
    vmem = pl.BlockSpec(memory_space=pltpu.VMEM)
    return pl.pallas_call(
        functools.partial(order_kernel, order),
        out_shape=jax.ShapeDtypeStruct((rows, 64 * len(order)), BF16),
        in_specs=[pl.BlockSpec(memory_space=pltpu.SMEM)] + [vmem] * len(sources),
        out_specs=vmem,
        compiler_params=pltpu.CompilerParams(vmem_limit_bytes=24 << 20),
        cost_estimate=pl.CostEstimate(flops=0, bytes_accessed=weight * 4 * rows * depth, transcendentals=0),
    )(bits, *sources)


def add_products(total, features, at, pieces):
    for piece in pieces:
        rows = piece.shape[0]
        term = jnp.dot(features[:, at:at + rows], piece[...], preferred_element_type=F32)
        total = term if total is None else total + term
        at += rows
    return total


def first_kernel(features, *refs):
    pieces, out = refs[:-1], refs[-1]
    out[...] = add_products(None, features, 0, pieces)


def last_kernel(at, keep, features, so_far, *refs):
    pieces, (kept, sent) = refs[:-2], refs[-2:]
    total = add_products(so_far[...], features, at, pieces)
    rows = total.shape[0] // (2 * keep)
    for i in range(keep):
        kept[i * rows:(i + 1) * rows, :] = total[2 * i * rows:(2 * i + 1) * rows]
        sent[i * rows:(i + 1) * rows, :] = total[(2 * i + 1) * rows:(2 * i + 2) * rows]


def project(features, pieces, late, keep, weight):
    rows, depth = features.shape
    width = pieces[0].shape[1]
    vmem = pl.BlockSpec(memory_space=pltpu.VMEM)
    early = len(pieces) - late
    params = pltpu.CompilerParams(vmem_limit_bytes=24 << 20)
    done = sum(p.shape[0] for p in pieces[:early])

    def cost(deep):
        return pl.CostEstimate(flops=2 * rows * deep * width, bytes_accessed=2 * deep * (width + rows), transcendentals=0)

    so_far = pl.pallas_call(
        first_kernel,
        out_shape=jax.ShapeDtypeStruct((rows, width), F32),
        in_specs=[vmem] * (1 + early),
        out_specs=vmem,
        compiler_params=params,
        cost_estimate=cost(weight * done),
    )(features, *pieces[:early])
    return pl.pallas_call(
        functools.partial(last_kernel, done, keep),
        out_shape=[jax.ShapeDtypeStruct((rows // 2, width), F32)] * 2,
        in_specs=[vmem] * (2 + late),
        out_specs=[vmem, vmem],
        compiler_params=params,
        cost_estimate=cost(depth - done),
    )(features, so_far, *pieces[early:])


def after(first, *then):
    return lax.optimization_barrier((first,) + then)[1:]


def attend_kernel(earlier, scalars, mine, pair, prefix, seg_col, *refs):
    blocks, out, q_all = refs[:earlier + 1], refs[earlier + 1], refs[earlier + 2]
    half = scalars[0]
    rows = mine.shape[0]
    q_all[half] = mine[...]
    q_all[1 - half] = pair[...]
    biases = []
    q_seg = seg_col[...]
    for i, block in enumerate(blocks):
        k_seg = block[rows:rows + 1, :rows].astype(F32)
        seen = q_seg == k_seg
        if i == 0:
            q_at = lax.broadcasted_iota(jnp.int32, (rows, rows), 0)
            k_at = lax.broadcasted_iota(jnp.int32, (rows, rows), 1)
            seen = seen & (k_at <= q_at)
            biases.append(jnp.where(seen, 0.0, NEG))
        else:
            biases.append(jnp.where(seen, jnp.where(scalars[1 + i] == 0, 0.0, NEG), NEG))
    bias = jnp.concatenate(biases, axis=1)
    bias = jnp.concatenate([bias] * REPEATS, axis=0)
    for head in range(KEY_HEADS):
        cols, vcols = slice(head * HD, (head + 1) * HD), slice(KVW + head * HD, KVW + (head + 1) * HD)
        base = head * REPEATS * HD
        heads = [divmod(head * REPEATS + r, QH // HD) for r in range(REPEATS)]
        queries = jnp.concatenate([q_all[part, :, h * HD:(h + 1) * HD] for part, h in heads], axis=0)
        keys = jnp.concatenate([block[:rows, cols] for block in blocks], axis=0)
        values = jnp.concatenate([block[:rows, vcols] for block in blocks], axis=0)
        contract = (((1,), (1,)), ((), ()))
        s_pre = lax.dot_general(queries, prefix[:, cols], contract, preferred_element_type=F32)
        s_suf = lax.dot_general(queries, keys, contract, preferred_element_type=F32) + bias
        top = jnp.maximum(jnp.max(s_pre, axis=-1, keepdims=True), jnp.max(s_suf, axis=-1, keepdims=True))
        p_pre, p_suf = jnp.exp(s_pre - top), jnp.exp(s_suf - top)
        total = jnp.sum(p_pre, axis=-1, keepdims=True) + jnp.sum(p_suf, axis=-1, keepdims=True)
        numerator = jnp.dot(p_pre.astype(BF16), prefix[:, vcols], preferred_element_type=F32)
        numerator += jnp.dot(p_suf.astype(BF16), values, preferred_element_type=F32)
        context = (numerator / total).astype(BF16)
        for r in range(REPEATS):
            out[:, base + r * HD:base + (r + 1) * HD] = context[r * rows:(r + 1) * rows]


def attend(halves, prefix, seg_col, blocks, scalars):
    rows = halves[0].shape[0]
    earlier = len(blocks) - 1
    vmem = pl.BlockSpec(memory_space=pltpu.VMEM)
    keys = prefix.shape[0] + rows * (earlier + 1)
    return pl.pallas_call(
        functools.partial(attend_kernel, earlier),
        out_shape=jax.ShapeDtypeStruct((rows, QW), BF16),
        in_specs=[pl.BlockSpec(memory_space=pltpu.SMEM)] + [vmem] * (4 + len(blocks)),
        out_specs=vmem,
        scratch_shapes=[pltpu.VMEM((2, rows, QH), BF16)],
        compiler_params=pltpu.CompilerParams(vmem_limit_bytes=40 << 20),
        cost_estimate=pl.CostEstimate(
            flops=4 * rows * keys * QW, bytes_accessed=4 * keys * KVW, transcendentals=rows * keys * QW // HD
        ),
    )(scalars, *halves, prefix, seg_col, *blocks)


def swap_body(tokens, norm_gain, w_qkv, prefix_kv, segments):
    inputs, seg_ids, own_prefix = tokens[0], segments[0], prefix_kv[0]
    rows = inputs.shape[0]
    gx, core, z, y = (lax.axis_index(a) for a in ("gx", "core", "z", "y"))
    z_count, y_count = lax.axis_size("z"), lax.axis_size("y")
    index = z * y_count + y
    depth = w_qkv.shape[0]

    have = {}

    def gate(point, *values):
        names = [n for n in ORDER.get(point, ()) if n in have]
        return after(tuple(have[n] for n in names), *values) if names else values

    kv_near = w_qkv[:, QW:]
    kv_zs = []
    for d in Z_ORDER:
        kv_zs.append(z_swap(*gate(f"kv_z{len(kv_zs)}", kv_near), d))
        have[f"kv_z{len(kv_zs) - 1}"] = kv_zs[-1]
    kv_near_sides = sides(*gate("kv_near_sides", kv_near))
    have["kv_near_sides"] = kv_near_sides

    pair = z & 1
    (w_own,) = gate("q_rows", w_qkv)
    q_got = z_swap(
        jnp.concatenate(
            [lax.dynamic_slice_in_dim(w_own, (1 - pair) * QH, QH, 1)] + ([own_prefix] if PREFIX_WITH_Q else [])
        ),
        1,
    )
    have["q_got"] = q_got
    q_near = jnp.concatenate([lax.dynamic_slice_in_dim(w_own, pair * QH, QH, 1), q_got[:depth]])

    kv_far = jnp.concatenate(gate("kv_far", *kv_zs))
    have["kv_far"] = kv_far
    kv_far_sides = sides(kv_far)
    have["kv_far_sides"] = kv_far_sides

    (normed_in,) = gate("norm", inputs)
    normed = rms_norm(normed_in, norm_gain)
    normed_sibling = swap(normed, "core")
    have["normed_sibling"] = normed_sibling
    number = ((gx * 2 + core) * z_count + z) * y_count + y
    bits = jnp.stack([(number >> i) & 1 for i in range(5)]).astype(jnp.int32)
    zs = (0,) + tuple(Z_ORDER)

    def blocks_at(dx, dy, dzs):
        return [(dx * 8 + dz) * 2 + dy for dz in dzs]

    kv_order = []
    for dx, dy, dzs in (
        (0, 0, zs[:1]), (1, 0, zs[:1]), (0, 1, zs[:1]), (0, 0, zs[1:]), (1, 0, zs[1:]), (0, 1, zs[1:]), (1, 1, zs)
    ):
        kv_order += blocks_at(dx, dy, dzs)
    kv_features = order_features([normed, normed_sibling], kv_order, bits, WEIGHT[0])
    have["kv_features"] = kv_features

    (q_load,) = gate("q_across", q_near)
    if PREFIX_WITH_Q == 1:
        q_load = jnp.concatenate([q_load, own_prefix, q_got[depth:]])
    q_across = z_swap(q_load, 2)
    have["q_across"] = q_across
    normed_pair = z_swap(*gate("normed_pair", normed), 1)
    have["normed_pair"] = normed_pair

    near_x, far_x, far_y = gate("kv_corner", kv_near_sides[0], *kv_far_sides)
    kv_low = swap(jnp.concatenate([near_x, far_x[:depth]]), "y")
    kv_high = swap(far_y[depth:], "gx")
    have["kv_corner"] = (kv_low, kv_high)
    if not PREFIX_WITH_Q:
        (line,) = gate("prefix_z1", own_prefix)
        line = jnp.concatenate([line, z_swap(line, 1)])
        have["prefix_z1"] = line
    kv_pieces = [kv_near, *kv_near_sides, kv_far, *kv_far_sides, *gate("kv_last", kv_low, kv_high)]
    kv_kept, kv_sent = project(kv_features, kv_pieces, 2, 1, WEIGHT[2])
    have["kv_theirs"] = kv_sent
    kv_other = swap(*gate("kv_other", kv_sent), "core")
    have["kv_other"] = kv_other
    q_line = jnp.concatenate([q_near, *gate("q_line", q_across[:2 * depth])])
    q_line_x, q_line_y = sides(q_line)
    have["q_sides"] = (q_line_x, q_line_y)
    seg_row = jnp.pad(seg_ids.astype(BF16)[None, :], ((0, 7), (0, 2 * KVW - rows)))
    block = jnp.concatenate([(kv_kept + kv_other).astype(BF16), seg_row], axis=0)
    have["block"] = block
    if PREFIX_WITH_Q == 1:
        line = jnp.concatenate([own_prefix, q_got[depth:], q_across[2 * depth:]])
    else:
        if PREFIX_WITH_Q:
            line = jnp.concatenate([own_prefix, q_got[depth:]])
        (line,) = gate("prefix_z2", line)
        line = jnp.concatenate([line, z_swap(line, 2)])
    have["prefix_z2"] = line

    q_order = []
    for dx, dy in ((0, 0), (1, 0), (0, 1), (1, 1)):
        q_order += blocks_at(dx, dy, (0, 1, 2, 3))
    (normed_pair,) = gate("diagonal", normed_pair)
    normed_diagonal = swap(normed_pair, "core")
    q_features = order_features([normed, normed_sibling, normed_pair, normed_diagonal], q_order, bits, WEIGHT[1])
    have["q_features"] = q_features

    upward = [(i, i + 1) for i in range(z_count - 1)]
    two_back = lax.ppermute(*gate("two_back", block), "z", upward)
    have["two_back"] = two_back
    prefix = jnp.concatenate([line, swap(*gate("prefix_y", line), "y")])
    have["prefix_y"] = prefix
    four_back = lax.ppermute(*gate("four_back", two_back), "z", upward)
    have["four_back"] = four_back
    odd_a = swap(*gate("odd_a", two_back), "y")
    have["odd_a"] = odd_a

    q_late_x, q_late_y = gate("q_corner", q_line_x, q_line_y)
    if CORNER_BY_X:
        q_corners = [swap(q_late_y, "gx")]
    else:
        q_corners = [swap(q_late_x[:2 * depth], "y"), swap(q_late_y[2 * depth:], "gx")]
    have["q_corner"] = q_corners
    odd_b = swap(*gate("odd_b", jnp.where(y == 0, block, four_back)), "y")
    have["odd_b"] = odd_b
    blocks = [block, two_back, four_back, odd_a, odd_b]
    distances = [0, 2, 4, 1 + 2 * y, 3 - 2 * y]

    q_pieces = [q_line, q_line_x, q_line_y, *gate("q_last", *q_corners)]
    q_kept, q_sent = project(q_features, q_pieces, len(q_corners), 2, WEIGHT[3])
    queries = (q_kept + swap(q_sent, "core")).astype(BF16) * jnp.asarray(0.125, BF16)
    halves = [queries[:rows], z_swap(*gate("q_res", queries[rows:]), 1)]

    scalars = jnp.stack([pair] + [jnp.where(index >= d, 0, 1) for d in distances]).astype(jnp.int32)
    context = attend(halves, prefix, seg_ids.astype(F32)[:, None], blocks, scalars)
    return context[None]


def gather_body(tokens, norm_gain, w_qkv, prefix_kv, segments):
    inputs, seg_ids = tokens[0], segments[0]
    rows = inputs.shape[0]
    normed = rms_norm(inputs, norm_gain)
    weights = lax.all_gather(w_qkv, ("gx", "core", "z", "y"), axis=0, tiled=True)
    projected = jnp.dot(normed, weights, preferred_element_type=F32).astype(BF16)
    queries = projected[:, :QW].reshape(rows, KEY_HEADS, REPEATS, HD)

    def absorb(state, keyvals, visible):
        running_max, denominator, numerator = state
        count = keyvals.shape[0]
        key_part = keyvals[:, :KVW].reshape(count, KEY_HEADS, HD)
        value_part = keyvals[:, KVW:].reshape(count, KEY_HEADS, HD)
        scores = jnp.einsum("tgrd,ngd->tgrn", queries, key_part, preferred_element_type=F32) * 0.125
        if visible is not None:
            scores = jnp.where(visible[:, None, None, :], scores, F32(NEG))
        new_max = jnp.maximum(running_max, jnp.max(scores, axis=-1))
        probability = jnp.exp(scores - new_max[..., None])
        if visible is not None:
            probability = jnp.where(visible[:, None, None, :], probability, F32(0.0))
        factor = jnp.exp(running_max - new_max)
        denominator = denominator * factor + jnp.sum(probability, axis=-1)
        numerator = numerator * factor[..., None] + jnp.einsum(
            "tgrn,ngd->tgrd", probability.astype(BF16), value_part, preferred_element_type=F32
        )
        return new_max, denominator, numerator

    def sweep(state, keyvals, key_seg):
        length = min(keyvals.shape[0], 512)

        def step(i, running):
            start = i * length
            part = lax.dynamic_slice_in_dim(keyvals, start, length, 0)
            if key_seg is None:
                return absorb(running, part, None)
            seg_part = lax.dynamic_slice_in_dim(key_seg, start, length, 0)
            key_pos = start + jnp.arange(length, dtype=jnp.int32)
            visible = (seg_part[None, :] == seg_ids[:, None]) & (key_pos[None, :] <= query_pos[:, None])
            return absorb(running, part, visible)

        return lax.fori_loop(0, keyvals.shape[0] // length, step, state)

    query_pos = lax.axis_index(("z", "y")) * rows + jnp.arange(rows, dtype=jnp.int32)
    state = (
        jnp.full((rows, KEY_HEADS, REPEATS), NEG, F32),
        jnp.zeros((rows, KEY_HEADS, REPEATS), F32),
        jnp.zeros((rows, KEY_HEADS, REPEATS, HD), F32),
    )
    along = functools.partial(lax.all_gather, axis_name=("z", "y"), axis=0, tiled=True)
    state = sweep(state, along(prefix_kv[0]), None)
    _, denominator, numerator = sweep(state, along(projected[:, QW:]), along(seg_ids))
    return (numerator / denominator[..., None]).reshape(rows, QW).astype(BF16)[None]


def solution(mesh):
    groups, seqs = mesh.shape["group"], mesh.shape["seq"]
    chips, z_count = groups // 2, seqs // 2
    fine = Mesh(mesh.devices.reshape(chips, 2, z_count, 2), ("gx", "core", "z", "y"))
    group, seq = ("gx", "core"), ("z", "y")
    short = chips == 2 and z_count == SMALL
    return jax.shard_map(
        swap_body if short else gather_body,
        mesh=fine,
        in_specs=(P(group, seq, None), P(), P(group + seq, None), P(group, seq, None), P(group, seq)),
        out_specs=P(group, seq, None),
        check_vma=False,
    )
```

```python
import functools

import jax
import jax.numpy as jnp
from jax import lax
from jax.experimental import pallas as pl
from jax.experimental.pallas import tpu as pltpu
from jax.sharding import Mesh, PartitionSpec as P

HD = 64
QW = 1280
KVW = 320
KEY_HEADS = KVW // HD
REPEATS = QW // KVW
QH = QW // 2
NEG = -1e30
SMALL = 4
PREFIX_WITH_Q = 2
CORNER_BY_X = True
Z_ORDER = (1, 2, 3)
WEIGHT = (1, 1, 1, 1)
ORDER = {
    "kv_near_sides": ("kv_z0",),
    "kv_far": ("kv_near_sides", "kv_features", "q_got",),
    "q_across": ("kv_far",),
    "normed_pair": ("kv_near_sides",),
    "kv_corner": ("kv_features",),
    "q_line": ("kv_far_sides",),
    "q_res": ("four_back", "odd_a",),
    "prefix_z1": ("kv_far_sides",),
    "prefix_z2": ("q_across",),
    "q_corner": ("two_back",),
    "four_back": ("normed_pair", "prefix_z2", "q_features",),
    "q_last": ("four_back", "prefix_y", "odd_a",),
}
F32 = jnp.float32
BF16 = jnp.bfloat16


def rms_norm(inputs, norm_gain):
    values = inputs.astype(F32)
    mean_square = jnp.mean(values * values, axis=-1, keepdims=True)
    return (values * lax.rsqrt(mean_square + 1e-05) * norm_gain.astype(F32)).astype(BF16)


def swap(x, axis):
    return lax.ppermute(x, axis, [(0, 1), (1, 0)])


def z_swap(x, distance):
    return lax.ppermute(x, "z", [(i, i ^ distance) for i in range(4)])


def sides(piece):
    return swap(piece, "gx"), swap(piece, "y")


def order_kernel(order, bits, *refs):
    sources, out = refs[:-1], refs[-1]
    at = 0
    for source in sources:
        rows, depth = source.shape
        x = source[...]
        for bit in range((depth // 64).bit_length() - 1):
            span = 64 << bit
            parts = [x[:, (i ^ 1) * span:((i ^ 1) + 1) * span] for i in range(depth // span)]
            x = jnp.where(bits[bit] == 1, jnp.concatenate(parts, axis=1), x)
        out[at:at + rows, :] = jnp.concatenate([x[:, b * 64:(b + 1) * 64] for b in order], axis=1)
        at += rows


def order_features(sources, order, bits, weight):
    depth = sources[0].shape[1]
    rows = sum(x.shape[0] for x in sources)
    vmem = pl.BlockSpec(memory_space=pltpu.VMEM)
    return pl.pallas_call(
        functools.partial(order_kernel, order),
        out_shape=jax.ShapeDtypeStruct((rows, 64 * len(order)), BF16),
        in_specs=[pl.BlockSpec(memory_space=pltpu.SMEM)] + [vmem] * len(sources),
        out_specs=vmem,
        compiler_params=pltpu.CompilerParams(vmem_limit_bytes=24 << 20),
        cost_estimate=pl.CostEstimate(flops=0, bytes_accessed=weight * 4 * rows * depth, transcendentals=0),
    )(bits, *sources)


def add_products(total, features, at, pieces):
    for piece in pieces:
        rows = piece.shape[0]
        term = jnp.dot(features[:, at:at + rows], piece[...], preferred_element_type=F32)
        total = term if total is None else total + term
        at += rows
    return total


def first_kernel(features, *refs):
    pieces, out = refs[:-1], refs[-1]
    out[...] = add_products(None, features, 0, pieces)


def last_kernel(at, keep, features, so_far, *refs):
    pieces, (kept, sent) = refs[:-2], refs[-2:]
    total = add_products(so_far[...], features, at, pieces)
    rows = total.shape[0] // (2 * keep)
    for i in range(keep):
        kept[i * rows:(i + 1) * rows, :] = total[2 * i * rows:(2 * i + 1) * rows]
        sent[i * rows:(i + 1) * rows, :] = total[(2 * i + 1) * rows:(2 * i + 2) * rows]


def project(features, pieces, late, keep, weight):
    rows, depth = features.shape
    width = pieces[0].shape[1]
    vmem = pl.BlockSpec(memory_space=pltpu.VMEM)
    early = len(pieces) - late
    params = pltpu.CompilerParams(vmem_limit_bytes=24 << 20)
    done = sum(p.shape[0] for p in pieces[:early])

    def cost(deep):
        return pl.CostEstimate(flops=2 * rows * deep * width, bytes_accessed=2 * deep * (width + rows), transcendentals=0)

    so_far = pl.pallas_call(
        first_kernel,
        out_shape=jax.ShapeDtypeStruct((rows, width), F32),
        in_specs=[vmem] * (1 + early),
        out_specs=vmem,
        compiler_params=params,
        cost_estimate=cost(weight * done),
    )(features, *pieces[:early])
    return pl.pallas_call(
        functools.partial(last_kernel, done, keep),
        out_shape=[jax.ShapeDtypeStruct((rows // 2, width), F32)] * 2,
        in_specs=[vmem] * (2 + late),
        out_specs=[vmem, vmem],
        compiler_params=params,
        cost_estimate=cost(depth - done),
    )(features, so_far, *pieces[early:])


def after(first, *then):
    return lax.optimization_barrier((first,) + then)[1:]


def attend_kernel(earlier, scalars, mine, pair, prefix, seg_col, *refs):
    blocks, out, q_all = refs[:earlier + 1], refs[earlier + 1], refs[earlier + 2]
    half = scalars[0]
    rows = mine.shape[0]
    q_all[half] = mine[...]
    q_all[1 - half] = pair[...]
    biases = []
    q_seg = seg_col[...]
    for i, block in enumerate(blocks):
        k_seg = block[rows:rows + 1, :rows].astype(F32)
        seen = q_seg == k_seg
        if i == 0:
            q_at = lax.broadcasted_iota(jnp.int32, (rows, rows), 0)
            k_at = lax.broadcasted_iota(jnp.int32, (rows, rows), 1)
            seen = seen & (k_at <= q_at)
            biases.append(jnp.where(seen, 0.0, NEG))
        else:
            biases.append(jnp.where(seen, jnp.where(scalars[1 + i] == 0, 0.0, NEG), NEG))
    bias = jnp.concatenate(biases, axis=1)
    bias = jnp.concatenate([bias] * REPEATS, axis=0)
    for head in range(KEY_HEADS):
        cols, vcols = slice(head * HD, (head + 1) * HD), slice(KVW + head * HD, KVW + (head + 1) * HD)
        base = head * REPEATS * HD
        heads = [divmod(head * REPEATS + r, QH // HD) for r in range(REPEATS)]
        queries = jnp.concatenate([q_all[part, :, h * HD:(h + 1) * HD] for part, h in heads], axis=0)
        keys = jnp.concatenate([prefix[:, cols]] + [block[:rows, cols] for block in blocks], axis=0)
        values = jnp.concatenate([prefix[:, vcols]] + [block[:rows, vcols] for block in blocks], axis=0)
        contract = (((1,), (1,)), ((), ()))
        scores = lax.dot_general(queries, keys, contract, preferred_element_type=F32)
        count = prefix.shape[0]
        s_pre, s_suf = scores[:, :count], scores[:, count:] + bias
        top = jnp.maximum(jnp.max(s_pre, axis=-1, keepdims=True), jnp.max(s_suf, axis=-1, keepdims=True))
        p_pre, p_suf = jnp.exp(s_pre - top), jnp.exp(s_suf - top)
        total = jnp.sum(p_pre, axis=-1, keepdims=True) + jnp.sum(p_suf, axis=-1, keepdims=True)
        rounded = jnp.concatenate([p_pre.astype(BF16), p_suf.astype(BF16)], axis=1)
        numerator = jnp.dot(rounded, values, preferred_element_type=F32)
        context = (numerator / total).astype(BF16)
        for r in range(REPEATS):
            out[:, base + r * HD:base + (r + 1) * HD] = context[r * rows:(r + 1) * rows]


def attend(halves, prefix, seg_col, blocks, scalars):
    rows = halves[0].shape[0]
    earlier = len(blocks) - 1
    vmem = pl.BlockSpec(memory_space=pltpu.VMEM)
    keys = prefix.shape[0] + rows * (earlier + 1)
    return pl.pallas_call(
        functools.partial(attend_kernel, earlier),
        out_shape=jax.ShapeDtypeStruct((rows, QW), BF16),
        in_specs=[pl.BlockSpec(memory_space=pltpu.SMEM)] + [vmem] * (4 + len(blocks)),
        out_specs=vmem,
        scratch_shapes=[pltpu.VMEM((2, rows, QH), BF16)],
        compiler_params=pltpu.CompilerParams(vmem_limit_bytes=40 << 20),
        cost_estimate=pl.CostEstimate(
            flops=4 * rows * keys * QW, bytes_accessed=4 * keys * KVW, transcendentals=rows * keys * QW // HD
        ),
    )(scalars, *halves, prefix, seg_col, *blocks)


def swap_body(tokens, norm_gain, w_qkv, prefix_kv, segments):
    inputs, seg_ids, own_prefix = tokens[0], segments[0], prefix_kv[0]
    rows = inputs.shape[0]
    gx, core, z, y = (lax.axis_index(a) for a in ("gx", "core", "z", "y"))
    z_count, y_count = lax.axis_size("z"), lax.axis_size("y")
    index = z * y_count + y
    depth = w_qkv.shape[0]

    have = {}

    def gate(point, *values):
        names = [n for n in ORDER.get(point, ()) if n in have]
        return after(tuple(have[n] for n in names), *values) if names else values

    kv_near = w_qkv[:, QW:]
    kv_zs = []
    for d in Z_ORDER:
        kv_zs.append(z_swap(*gate(f"kv_z{len(kv_zs)}", kv_near), d))
        have[f"kv_z{len(kv_zs) - 1}"] = kv_zs[-1]
    kv_near_sides = sides(*gate("kv_near_sides", kv_near))
    have["kv_near_sides"] = kv_near_sides

    pair = z & 1
    (w_own,) = gate("q_rows", w_qkv)
    q_got = z_swap(
        jnp.concatenate(
            [lax.dynamic_slice_in_dim(w_own, (1 - pair) * QH, QH, 1)] + ([own_prefix] if PREFIX_WITH_Q else [])
        ),
        1,
    )
    have["q_got"] = q_got
    q_near = jnp.concatenate([lax.dynamic_slice_in_dim(w_own, pair * QH, QH, 1), q_got[:depth]])

    kv_far = jnp.concatenate(gate("kv_far", *kv_zs))
    have["kv_far"] = kv_far
    kv_far_sides = sides(kv_far)
    have["kv_far_sides"] = kv_far_sides

    (normed_in,) = gate("norm", inputs)
    normed = rms_norm(normed_in, norm_gain)
    normed_sibling = swap(normed, "core")
    have["normed_sibling"] = normed_sibling
    number = ((gx * 2 + core) * z_count + z) * y_count + y
    bits = jnp.stack([(number >> i) & 1 for i in range(5)]).astype(jnp.int32)
    zs = (0,) + tuple(Z_ORDER)

    def blocks_at(dx, dy, dzs):
        return [(dx * 8 + dz) * 2 + dy for dz in dzs]

    kv_order = []
    for dx, dy, dzs in (
        (0, 0, zs[:1]), (1, 0, zs[:1]), (0, 1, zs[:1]), (0, 0, zs[1:]), (1, 0, zs[1:]), (0, 1, zs[1:]), (1, 1, zs)
    ):
        kv_order += blocks_at(dx, dy, dzs)
    kv_features = order_features([normed, normed_sibling], kv_order, bits, WEIGHT[0])
    have["kv_features"] = kv_features

    (q_load,) = gate("q_across", q_near)
    if PREFIX_WITH_Q == 1:
        q_load = jnp.concatenate([q_load, own_prefix, q_got[depth:]])
    q_across = z_swap(q_load, 2)
    have["q_across"] = q_across
    normed_pair = z_swap(*gate("normed_pair", normed), 1)
    have["normed_pair"] = normed_pair

    near_x, far_x, far_y = gate("kv_corner", kv_near_sides[0], *kv_far_sides)
    kv_low = swap(jnp.concatenate([near_x, far_x[:depth]]), "y")
    kv_high = swap(far_y[depth:], "gx")
    have["kv_corner"] = (kv_low, kv_high)
    if not PREFIX_WITH_Q:
        (line,) = gate("prefix_z1", own_prefix)
        line = jnp.concatenate([line, z_swap(line, 1)])
        have["prefix_z1"] = line
    kv_pieces = [kv_near, *kv_near_sides, kv_far, *kv_far_sides, *gate("kv_last", kv_low, kv_high)]
    kv_kept, kv_sent = project(kv_features, kv_pieces, 2, 1, WEIGHT[2])
    have["kv_theirs"] = kv_sent
    kv_other = swap(*gate("kv_other", kv_sent), "core")
    have["kv_other"] = kv_other
    q_line = jnp.concatenate([q_near, *gate("q_line", q_across[:2 * depth])])
    q_line_x, q_line_y = sides(q_line)
    have["q_sides"] = (q_line_x, q_line_y)
    seg_row = jnp.pad(seg_ids.astype(BF16)[None, :], ((0, 7), (0, 2 * KVW - rows)))
    block = jnp.concatenate([(kv_kept + kv_other).astype(BF16), seg_row], axis=0)
    have["block"] = block
    if PREFIX_WITH_Q == 1:
        line = jnp.concatenate([own_prefix, q_got[depth:], q_across[2 * depth:]])
    else:
        if PREFIX_WITH_Q:
            line = jnp.concatenate([own_prefix, q_got[depth:]])
        (line,) = gate("prefix_z2", line)
        line = jnp.concatenate([line, z_swap(line, 2)])
    have["prefix_z2"] = line

    q_order = []
    for dx, dy in ((0, 0), (1, 0), (0, 1), (1, 1)):
        q_order += blocks_at(dx, dy, (0, 1, 2, 3))
    (normed_pair,) = gate("diagonal", normed_pair)
    normed_diagonal = swap(normed_pair, "core")
    q_features = order_features([normed, normed_sibling, normed_pair, normed_diagonal], q_order, bits, WEIGHT[1])
    have["q_features"] = q_features

    upward = [(i, i + 1) for i in range(z_count - 1)]
    two_back = lax.ppermute(*gate("two_back", block), "z", upward)
    have["two_back"] = two_back
    prefix = jnp.concatenate([line, swap(*gate("prefix_y", line), "y")])
    have["prefix_y"] = prefix
    four_back = lax.ppermute(*gate("four_back", two_back), "z", upward)
    have["four_back"] = four_back
    odd_a = swap(*gate("odd_a", two_back), "y")
    have["odd_a"] = odd_a

    q_late_x, q_late_y = gate("q_corner", q_line_x, q_line_y)
    if CORNER_BY_X:
        q_corners = [swap(q_late_y, "gx")]
    else:
        q_corners = [swap(q_late_x[:2 * depth], "y"), swap(q_late_y[2 * depth:], "gx")]
    have["q_corner"] = q_corners
    odd_b = swap(*gate("odd_b", jnp.where(y == 0, block, four_back)), "y")
    have["odd_b"] = odd_b
    blocks = [block, two_back, four_back, odd_a, odd_b]
    distances = [0, 2, 4, 1 + 2 * y, 3 - 2 * y]

    q_pieces = [q_line, q_line_x, q_line_y, *gate("q_last", *q_corners)]
    q_kept, q_sent = project(q_features, q_pieces, len(q_corners), 2, WEIGHT[3])
    queries = (q_kept + swap(q_sent, "core")).astype(BF16) * jnp.asarray(0.125, BF16)
    halves = [queries[:rows], z_swap(*gate("q_res", queries[rows:]), 1)]

    scalars = jnp.stack([pair] + [jnp.where(index >= d, 0, 1) for d in distances]).astype(jnp.int32)
    context = attend(halves, prefix, seg_ids.astype(F32)[:, None], blocks, scalars)
    return context[None]


def gather_body(tokens, norm_gain, w_qkv, prefix_kv, segments):
    inputs, seg_ids = tokens[0], segments[0]
    rows = inputs.shape[0]
    normed = rms_norm(inputs, norm_gain)
    weights = lax.all_gather(w_qkv, ("gx", "core", "z", "y"), axis=0, tiled=True)
    projected = jnp.dot(normed, weights, preferred_element_type=F32).astype(BF16)
    queries = projected[:, :QW].reshape(rows, KEY_HEADS, REPEATS, HD)

    def absorb(state, keyvals, visible):
        running_max, denominator, numerator = state
        count = keyvals.shape[0]
        key_part = keyvals[:, :KVW].reshape(count, KEY_HEADS, HD)
        value_part = keyvals[:, KVW:].reshape(count, KEY_HEADS, HD)
        scores = jnp.einsum("tgrd,ngd->tgrn", queries, key_part, preferred_element_type=F32) * 0.125
        if visible is not None:
            scores = jnp.where(visible[:, None, None, :], scores, F32(NEG))
        new_max = jnp.maximum(running_max, jnp.max(scores, axis=-1))
        probability = jnp.exp(scores - new_max[..., None])
        if visible is not None:
            probability = jnp.where(visible[:, None, None, :], probability, F32(0.0))
        factor = jnp.exp(running_max - new_max)
        denominator = denominator * factor + jnp.sum(probability, axis=-1)
        numerator = numerator * factor[..., None] + jnp.einsum(
            "tgrn,ngd->tgrd", probability.astype(BF16), value_part, preferred_element_type=F32
        )
        return new_max, denominator, numerator

    def sweep(state, keyvals, key_seg):
        length = min(keyvals.shape[0], 512)

        def step(i, running):
            start = i * length
            part = lax.dynamic_slice_in_dim(keyvals, start, length, 0)
            if key_seg is None:
                return absorb(running, part, None)
            seg_part = lax.dynamic_slice_in_dim(key_seg, start, length, 0)
            key_pos = start + jnp.arange(length, dtype=jnp.int32)
            visible = (seg_part[None, :] == seg_ids[:, None]) & (key_pos[None, :] <= query_pos[:, None])
            return absorb(running, part, visible)

        return lax.fori_loop(0, keyvals.shape[0] // length, step, state)

    query_pos = lax.axis_index(("z", "y")) * rows + jnp.arange(rows, dtype=jnp.int32)
    state = (
        jnp.full((rows, KEY_HEADS, REPEATS), NEG, F32),
        jnp.zeros((rows, KEY_HEADS, REPEATS), F32),
        jnp.zeros((rows, KEY_HEADS, REPEATS, HD), F32),
    )
    along = functools.partial(lax.all_gather, axis_name=("z", "y"), axis=0, tiled=True)
    state = sweep(state, along(prefix_kv[0]), None)
    _, denominator, numerator = sweep(state, along(projected[:, QW:]), along(seg_ids))
    return (numerator / denominator[..., None]).reshape(rows, QW).astype(BF16)[None]


def solution(mesh):
    groups, seqs = mesh.shape["group"], mesh.shape["seq"]
    chips, z_count = groups // 2, seqs // 2
    fine = Mesh(mesh.devices.reshape(chips, 2, z_count, 2), ("gx", "core", "z", "y"))
    group, seq = ("gx", "core"), ("z", "y")
    short = chips == 2 and z_count == SMALL
    return jax.shard_map(
        swap_body if short else gather_body,
        mesh=fine,
        in_specs=(P(group, seq, None), P(), P(group + seq, None), P(group, seq, None), P(group, seq)),
        out_specs=P(group, seq, None),
        check_vma=False,
    )
```
